32 devices in a mesh: ctx: 8 (over y, x, core), fsdp: 4 (over z).
Axes of the slice: x: 2, y: 2, z: 4, core: 2. Of those that a mesh axis runs over, the one named last changes fastest.
Arguments:
- hidden_in: bfloat16 [4, 1024, 2048], P('fsdp', 'ctx'), may hold values from -6 to 6
- out_cotangent: bfloat16 [4, 1024, 2048], P('fsdp', 'ctx'), may hold values from -6 to 6
- seq_lengths: int32 [4], P('fsdp'), may hold values from 256 to 1024, as said below
- first_gain: bfloat16 [2048], P(('ctx', 'fsdp')), may hold values from 0.25 to 1.75
- first_shift: bfloat16 [2048], P(('ctx', 'fsdp')), may hold values from -1.75 to 1.75
- qkv_weight: bfloat16 [2048, 2304], P(('ctx', 'fsdp')), may hold values from -0.125 to 0.125
- query_bias: bfloat16 [2048], P(('ctx', 'fsdp')), may hold values from -3 to 3
- value_bias: bfloat16 [128], P(('ctx', 'fsdp')), may hold values from -0.1875 to 0.1875
- proj_weight: bfloat16 [2048, 2048], P(('ctx', 'fsdp')), may hold values from -2 to 2
- proj_bias: bfloat16 [2048], P(('ctx', 'fsdp')), may hold values from -3.5 to 3.5
- second_gain: bfloat16 [2048], P(('ctx', 'fsdp')), may hold values from 0.25 to 1.75
- second_shift: bfloat16 [2048], P(('ctx', 'fsdp')), may hold values from -1.75 to 1.75
- up_weight: bfloat16 [2048, 8192], P(('ctx', 'fsdp')), may hold values from -0.125 to 0.125
- up_bias: bfloat16 [8192], P(('ctx', 'fsdp')), may hold values from -3 to 3
- down_weight: bfloat16 [8192, 2048], P(('ctx', 'fsdp')), may hold values from -0.0625 to 0.0625
- down_bias: bfloat16 [2048], P(('ctx', 'fsdp')), may hold values from -3.5 to 3.5
Outputs:
- layer_out: bfloat16 [4, 1024, 2048], P('fsdp', 'ctx')
- input_grad: float32 [4, 1024, 2048], P('fsdp', 'ctx')
- first_gain_grad: float32 [2048], P(('ctx', 'fsdp'))
- first_shift_grad: float32 [2048], P(('ctx', 'fsdp'))
- qkv_weight_grad: float32 [2048, 2304], P(('ctx', 'fsdp'))
- query_bias_grad: float32 [2048], P(('ctx', 'fsdp'))
- value_bias_grad: float32 [128], P(('ctx', 'fsdp'))
- proj_weight_grad: float32 [2048, 2048], P(('ctx', 'fsdp'))
- proj_bias_grad: float32 [2048], P(('ctx', 'fsdp'))
- second_gain_grad: float32 [2048], P(('ctx', 'fsdp'))
- second_shift_grad: float32 [2048], P(('ctx', 'fsdp'))
- up_weight_grad: float32 [2048, 8192], P(('ctx', 'fsdp'))
- up_bias_grad: float32 [8192], P(('ctx', 'fsdp'))
- down_weight_grad: float32 [8192, 2048], P(('ctx', 'fsdp'))
- down_bias_grad: float32 [2048], P(('ctx', 'fsdp'))
The draws below stay inside these ranges and needn't reach their ends.
Inputs may be any that keep to these rules, and one draw needn't show every extreme that they name: `seq_lengths`: live positions of a sequence come first; in every draw some sequence is full (1024).
All inputs are finite; a program needn't handle non-finite values.
Results may differ from the reference program's by a relative error of at most 0.025.
Values may be sent and summed in bfloat16 or wider, within the bound.
No kernel may reach another device: no remote copies, remote signals or barrier semaphores. Data moves between devices by JAX's collectives and lax.ppermute only.
A program may use at most 384 MiB of HBM per device.

```python
import math
import jax
import jax.numpy as jnp
from jax import lax

D = 2048
HEADS = 16
HD = 128
FF = 8192
LENGTH = 1024
SEQS = 4


def draw_seq_lengths(key, part):
    first, second = jax.random.split(jax.random.fold_in(key, 17))
    drawn = jax.random.randint(first, (SEQS,), LENGTH // 4, LENGTH + 1)
    chosen = jax.random.randint(second, (), 0, SEQS)
    return jnp.where(jnp.arange(SEQS) == chosen, LENGTH, drawn).astype(jnp.int32)


def shard_levels(stream_key, shape, cuts, low, largest):
    level, own = 1.0, jax.random.fold_in(stream_key, 6)
    for axis_at, shards_of in cuts:
        steps = jnp.exp(jax.random.uniform(jax.random.fold_in(own, axis_at), (shards_of,), jnp.float32, low / len(cuts), largest / len(cuts)))
        level = level * jnp.repeat(steps, shape[axis_at] // shards_of).reshape([-1 if axis == axis_at else 1 for axis in range(len(shape))])
    return level


def noise(key, shape, width, most, cuts=(), held_as=jnp.bfloat16):
    level = shard_levels(key, shape, cuts, -0.22, 0.18) if cuts else 1.0
    values = jax.random.normal(key, shape, jnp.float32) * width * level
    return jnp.minimum(jnp.maximum(values, -most), most).astype(held_as)


def setup_inputs(seed: int = 0) -> dict:
    splits = jax.random.split(jax.random.key(seed), 17)
    return {
        "hidden_in": noise(splits[0], (SEQS, LENGTH, D), 1.0, 6.0, ((0, 4), (1, 8))),
        "out_cotangent": noise(splits[1], (SEQS, LENGTH, D), 1.0, 6.0, ((0, 4), (1, 8))),
        "seq_lengths": draw_seq_lengths(jax.random.fold_in(splits[16], 71), 0),
        "first_gain": jnp.clip(1.0 + 0.15 * jax.random.normal(splits[3], (D,), jnp.float32), 0.25, 1.75).astype(jnp.bfloat16),
        "first_shift": noise(splits[4], (D,), 0.3, 1.75, ((0, 32),)),
        "qkv_weight": noise(splits[5], (D, D + 2 * HD), D ** -0.5, 0.125, ((0, 32),)),
        "query_bias": noise(splits[6], (D,), 0.5, 3.0, ((0, 32),)),
        "value_bias": noise(splits[7], (HD,), 0.03, 0.1875, ((0, 32),)),
        "proj_weight": noise(splits[8], (D, D), (D // 256) ** -0.5, 2.0, ((0, 32),)),
        "proj_bias": noise(splits[9], (D,), 0.6, 3.5, ((0, 32),)),
        "second_gain": jnp.clip(1.0 + 0.15 * jax.random.normal(splits[10], (D,), jnp.float32), 0.25, 1.75).astype(jnp.bfloat16),
        "second_shift": noise(splits[11], (D,), 0.3, 1.75, ((0, 32),)),
        "up_weight": noise(splits[12], (D, FF), D ** -0.5, 0.125, ((0, 32),)),
        "up_bias": noise(splits[13], (FF,), 0.5, 3.0, ((0, 32),)),
        "down_weight": noise(splits[14], (FF, D), FF ** -0.5, 0.0625, ((0, 32),)),
        "down_bias": noise(splits[15], (D,), 0.6, 3.5, ((0, 32),)),
    }


EPS = 1e-05
HIGH_PRECISION = lax.Precision.HIGHEST

@jax.custom_vjp
def low(v):
    return lax.optimization_barrier(v.astype(jnp.bfloat16)).astype(jnp.float32)

@jax.custom_vjp
def low_back(v):
    return v

def low_keep(v):
    return (low(v), None)

def low_pass(kept, grad):
    return (grad,)

def back_keep(v):
    return (v, None)

def back_low(kept, grad):
    return (low(grad),)
low.defvjp(low_keep, low_pass)
low_back.defvjp(back_keep, back_low)

def layer_norm(values, gain, shift):
    center = values - lax.optimization_barrier(jnp.mean(values, -1, keepdims=True))
    return center * lax.rsqrt(lax.optimization_barrier(jnp.mean(center * center, -1, keepdims=True)) + EPS) * gain + shift

def matmul(left_operand, right_operand):
    return jnp.einsum('owy,yx->owx', left_operand, right_operand, precision=HIGH_PRECISION)

def attend_sequence(operands):
    queries, keys, values, length = operands
    block_rows = min(512, LENGTH)
    grouped = queries.reshape(LENGTH // block_rows, block_rows, HEADS, HD)
    starts = jnp.arange(LENGTH // block_rows, dtype=jnp.int32) * block_rows
    key_pos = jnp.arange(LENGTH, dtype=jnp.int32)
    scale = 1.0 / math.sqrt(HD)

    def one_block(item):
        block, start = item
        scores = jnp.einsum('qhe,ke->qhk', block, keys, precision=HIGH_PRECISION) * scale
        query_pos = start + jnp.arange(block_rows, dtype=jnp.int32)
        allowed = (key_pos[None, :] <= query_pos[:, None]) & (key_pos[None, :] < length)
        scores = low_back(jnp.where(allowed[:, None, :], scores, -1e+30))
        probs = jax.nn.softmax(scores, axis=-1)
        return jnp.einsum('qhk,ke->qhe', low(probs), values, precision=HIGH_PRECISION)
    return lax.map(jax.checkpoint(one_block), (grouped, starts)).reshape(LENGTH, HEADS * HD)

def layer(rows, lengths, gain_a, shift_a, qkv_w, query_b, value_b, proj_w, proj_b, gain_b, shift_b, up_w, up_b, down_w, down_b):
    normed = low(layer_norm(rows, gain_a, shift_a))
    mixed = matmul(normed, qkv_w)
    queries = low_back(low(mixed[..., :D] + query_b))
    keys = low_back(low(mixed[..., D:D + HD]))
    values = low_back(low(mixed[..., D + HD:] + value_b))
    attended = lax.map(jax.checkpoint(attend_sequence), (queries, keys, values, lengths))
    attended = low_back(low(attended))
    middle = rows + low_back(matmul(attended, proj_w) + proj_b)
    normed_two = low(layer_norm(middle, gain_b, shift_b))
    before = low_back(matmul(normed_two, up_w) + up_b)
    active = low(jax.nn.gelu(before, approximate=True))
    result = middle + low_back(matmul(active, down_w) + down_b)
    live = jnp.arange(LENGTH, dtype=jnp.int32)[None, :] < lengths[:, None]
    return jnp.where(live[..., None], result, 0.0)

def reference(hidden_in, out_cotangent, seq_lengths, first_gain, first_shift, qkv_weight, query_bias, value_bias, proj_weight, proj_bias, second_gain, second_shift, up_weight, up_bias, down_weight, down_bias):
    params = tuple((p.astype(jnp.float32) for p in (first_gain, first_shift, qkv_weight, query_bias, value_bias, proj_weight, proj_bias, second_gain, second_shift, up_weight, up_bias, down_weight, down_bias)))

    def forward(rows, *weights):
        return layer(rows, seq_lengths, *weights)
    output, pull = jax.vjp(forward, hidden_in.astype(jnp.float32), *params)
    grads = pull(out_cotangent.astype(jnp.float32))
    return (output.astype(jnp.bfloat16), grads[0], grads[1], grads[2], grads[3], grads[4], grads[5], grads[6], grads[7], grads[8], grads[9], grads[10], grads[11], grads[12], grads[13])
```

```python
import math

import jax
import jax.numpy as jnp
from jax import lax
from jax.sharding import PartitionSpec as P

HEADS = 16
HD = 128
EPS = 1e-05
NEG = -1e30
BOTH = ("ctx", "fsdp")
BF = jnp.bfloat16
F32 = jnp.float32


def dot(a, b, da, db):
    return lax.dot_general(
        a, b, (((da,), (db,)), ((), ())), preferred_element_type=F32
    )


def normalize(values):
    center = values - jnp.mean(values, -1, keepdims=True)
    inverse = lax.rsqrt(jnp.mean(center * center, -1, keepdims=True) + EPS)
    return center * inverse, inverse


def norm_backward(grad, scaled, inverse, gain):
    inner = grad * gain
    return inverse * (
        inner
        - jnp.mean(inner, -1, keepdims=True)
        - scaled * jnp.mean(inner * scaled, -1, keepdims=True)
    )


def gelu(values):
    return jax.nn.gelu(values, approximate=True)


def after(value, *first):
    return lax.optimization_barrier((value,) + first)[0]


def exchange(value, mask):
    count = lax.axis_size("ctx")
    return lax.ppermute(value, "ctx", [(i, i ^ mask) for i in range(count)])


def chip_groups():
    count = lax.axis_size("ctx")
    return [list(range(core, count, 2)) for core in range(2)]


def chip_devices():
    width = 2 * lax.axis_size("fsdp")
    total = lax.axis_size("ctx") * lax.axis_size("fsdp")
    return [list(range(at, at + width)) for at in range(0, total, width)]


def plane_pieces(value):
    chips = lax.axis_size("ctx") // 2
    return [value] + [exchange(value, 2 * k) for k in range(1, chips)]


def both_cores(pieces):
    return jnp.concatenate(pieces + [exchange(piece, 1) for piece in pieces], 0)


def plane_scatter(left, weight, dim):
    chips = lax.axis_size("ctx") // 2
    rows = left.shape[0] // (2 * chips)
    half = rows * chips
    other = exchange(dot(left[half:], weight, 1, dim).astype(BF), 1)

    def block(k):
        return dot(left[k * rows : (k + 1) * rows], weight, 1, dim) + other[
            k * rows : (k + 1) * rows
        ].astype(F32)

    arrived = [exchange(block(k).astype(BF), 2 * k) for k in range(1, chips)]
    total = block(0)
    for piece in arrived:
        total = total + piece.astype(F32)
    return total


def column_chain(value):
    depth = lax.axis_size("fsdp")
    at = lax.axis_index("fsdp")
    upward, downward = [value], [value]
    for s in range(1, depth):
        upward.append(
            lax.ppermute(upward[-1], "fsdp", [(i, i + 1) for i in range(s - 1, depth - 1)])
        )
        downward.append(
            lax.ppermute(downward[-1], "fsdp", [(i, i - 1) for i in range(1, depth - s + 1)])
        )
    return [value] + [
        jnp.where(at >= s, upward[s], downward[depth - s]) for s in range(1, depth)
    ]


def turned(value, by):
    depth = lax.axis_size("fsdp")
    return lax.ppermute(value, "fsdp", [(i, (i + by) % depth) for i in range(depth)])


def column_direct(value):
    depth = lax.axis_size("fsdp")
    return [value] + [turned(value, s) for s in range(1, depth)]


def column_scatter(left, weight, dim, chain):
    depth = lax.axis_size("fsdp")
    rows = left.shape[0] // (2 * depth)
    half = rows * depth
    other = exchange(dot(left[half:], weight, 1, dim).astype(BF), 1)

    def block(s):
        return dot(left[s * rows : (s + 1) * rows], weight, 1, dim) + other[
            s * rows : (s + 1) * rows
        ].astype(F32)

    if not chain:
        total = block(0)
        for s in range(1, depth):
            total = total + turned(block(s).astype(BF), -s).astype(F32)
        return total
    upward = downward = None
    for s in range(1, depth):
        rising, falling = block(s), block(depth - s)
        if upward is not None:
            rising = rising + upward.astype(F32)
            falling = falling + downward.astype(F32)
        upward = lax.ppermute(
            rising.astype(BF), "fsdp", [(i, i + 1) for i in range(min(s, depth - 1))]
        )
        downward = lax.ppermute(
            falling.astype(BF), "fsdp", [(i, i - 1) for i in range(max(depth - s, 1), depth)]
        )
    return block(0) + upward.astype(F32) + downward.astype(F32)


def pad_rows(flat, width):
    rows = -(-flat.shape[0] // width)
    rows = -(-rows // 8) * 8
    return jnp.pad(flat, (0, rows * width - flat.shape[0])).reshape(rows, width)


def body(
    hidden_in,
    out_cotangent,
    seq_lengths,
    first_gain,
    first_shift,
    qkv_weight,
    query_bias,
    value_bias,
    proj_weight,
    proj_bias,
    second_gain,
    second_shift,
    up_weight,
    up_bias,
    down_weight,
    down_bias,
):
    count, depth = lax.axis_size("ctx"), lax.axis_size("fsdp")
    chips = count // 2
    at, level = lax.axis_index("ctx"), lax.axis_index("fsdp")
    core = at % 2
    span, width = hidden_in.shape[1:]
    wrows = qkv_weight.shape[0]
    hidden = up_weight.shape[1]
    frows = down_weight.shape[0]
    share = HEADS // count
    qcols = share * HD
    wide_cols = qcols + HD
    scale = 1.0 / math.sqrt(HD)
    length = seq_lengths[0]
    own_rows = hidden_in[0].astype(F32)
    positions = at * span + jnp.arange(span, dtype=jnp.int32)
    live = (positions < length)[:, None]
    upstream = jnp.where(live, out_cotangent[0].astype(F32), 0.0)
    grad_mlp_own = upstream.astype(BF)

    small = [
        first_gain,
        first_shift,
        query_bias,
        value_bias,
        proj_bias,
        second_gain,
        second_shift,
        up_bias,
        down_bias,
    ]
    packed = pad_rows(jnp.concatenate(small), wide_cols)
    qpart = qkv_weight[:, :width].reshape(wrows, count, qcols).transpose(1, 0, 2)
    kvpart = qkv_weight[:, width:].reshape(wrows, 2, HD).transpose(1, 0, 2)
    kvpart = jnp.broadcast_to(kvpart[None], (chips, 2, wrows, HD)).reshape(count, wrows, HD)
    outgoing = jnp.concatenate(
        [
            jnp.concatenate([qpart, kvpart], 2),
            jnp.broadcast_to(packed[None], (count,) + packed.shape),
        ],
        1,
    )
    incoming = lax.all_to_all(outgoing, "ctx", 0, 0, tiled=True)
    attn_all = lax.all_gather(incoming, "fsdp", axis=0)
    hidden_own, proj_own = lax.optimization_barrier((hidden_in[0], proj_weight, incoming))[:2]
    row_pieces = plane_pieces(hidden_own)
    rows = both_cores(row_pieces).astype(F32)
    proj_local = lax.all_gather(proj_own, "fsdp", axis=0, tiled=True)
    down_own = after(down_weight, *row_pieces)
    down_pieces = plane_pieces(down_own)
    scaled_all, _ = normalize(rows)
    scaled_all, attn_all = lax.optimization_barrier((scaled_all, attn_all))
    attn_rows = attn_all.transpose(1, 0, 2, 3)
    qkv_local = attn_rows[:, :, :wrows].reshape(width, wide_cols)
    table = attn_rows[:, :, wrows:].reshape(count * depth, -1)
    vectors, offset = [], 0
    for piece in small:
        n = piece.shape[0]
        vectors.append(table[:, offset : offset + n].reshape(-1).astype(F32))
        offset += n
    gain_one, shift_one, qbias, vbias, pbias, gain_two, shift_two, ubias, dbias = vectors
    qbias = lax.dynamic_slice(qbias, (at * qcols,), (qcols,))
    ubias = lax.dynamic_slice(
        ubias.reshape(chips, 2 * depth, frows), (0, core * depth + level, 0), (chips, 1, frows)
    ).reshape(-1)

    up_parts = (
        after(up_weight, attn_all)
        .reshape(wrows, chips, 2 * depth, frows)
        .transpose(2, 0, 1, 3)
        .reshape(2 * depth, wrows, chips * frows)
    )
    up_parts = lax.all_to_all(
        up_parts, BOTH, 0, 0, tiled=True, axis_index_groups=chip_devices()
    ).reshape(2 * depth * wrows, chips * frows)
    mlp_pieces = column_direct(after(grad_mlp_own, up_parts))

    normed_one = (scaled_all * gain_one + shift_one).astype(BF)
    mixed = dot(normed_one, qkv_local, 1, 0)
    total = span * count
    queries = (mixed[:, :qcols] + qbias).astype(BF)
    mine = (mixed[:, qcols:] + jnp.where(core == 1, vbias, 0.0)).astype(BF)
    theirs = jnp.roll(exchange(mine, 1), total // 2, 0)
    keys = jnp.where(core == 0, mine, theirs)
    values = jnp.where(core == 0, theirs, mine)
    base = jnp.stack([at ^ (2 * k + j) for j in range(2) for k in range(chips)]) * span
    pos = (base[:, None] + jnp.arange(span, dtype=jnp.int32)[None]).reshape(total)
    allowed = (pos[None, :] <= pos[:, None]) & (pos[None, :] < length)
    heads = []
    attended_f = []
    for h in range(share):
        q = queries[:, h * HD : (h + 1) * HD]
        scores = jnp.where(allowed, dot(q, keys, 1, 1) * scale, NEG)
        top = jnp.max(scores, -1, keepdims=True)
        expo = jnp.where(allowed, jnp.exp(scores - top), 0.0)
        probs = expo / jnp.sum(expo, -1, keepdims=True)
        attended_f.append(dot(probs.astype(BF), values, 1, 0))
        heads.append((q, probs))
    attended = jnp.concatenate(attended_f, 1).astype(BF)
    branch = plane_scatter(attended, proj_local, 0)
    middle = own_rows + branch + pbias
    scaled_two, inverse_two = normalize(middle)
    normed_two_own = (scaled_two * gain_two + shift_two).astype(BF)

    up_local = lax.all_gather(
        after(up_parts, normed_two_own), "ctx", axis=0, tiled=True, axis_index_groups=chip_groups()
    )
    chip = at // 2
    down_local = jnp.zeros((chips, frows, width), BF)
    for k, piece in enumerate(down_pieces):
        down_local = lax.dynamic_update_slice(down_local, piece[None], (chip ^ k, 0, 0))
    down_local = down_local.reshape(chips * frows, width)
    grad_mlp = both_cores(mlp_pieces)
    grad_active = dot(grad_mlp, down_local, 1, 1)
    normed_two = both_cores(column_chain(normed_two_own))
    normed_two, grad_active = lax.optimization_barrier((normed_two, grad_active))
    before = dot(normed_two, up_local, 1, 0) + ubias
    active_f, gelu_pull = jax.vjp(gelu, before)
    active = active_f.astype(BF)
    grad_before = gelu_pull(grad_active)[0].astype(BF)
    ubias_term = jnp.sum(grad_before.astype(F32), 0)
    grad_two = column_scatter(grad_before, up_local, 1, True)

    def chip_sum(term):
        return lax.psum_scatter(
            term, "ctx", scatter_dimension=0, tiled=True, axis_index_groups=chip_groups()
        )

    down_term = dot(active, grad_mlp, 0, 0).astype(BF)
    up_term = dot(normed_two, grad_before, 0, 0).astype(BF)
    grad_two, down_term, up_term = lax.optimization_barrier((grad_two, down_term, up_term))
    down_grad = chip_sum(down_term)
    up_grad = chip_sum(up_term)
    gain_two_term = jnp.sum(grad_two * scaled_two, 0)
    shift_two_term = jnp.sum(grad_two, 0)
    grad_middle = upstream + norm_backward(grad_two, scaled_two, inverse_two, gain_two)
    grad_branch_own = grad_middle.astype(BF)
    pbias_term = jnp.sum(grad_branch_own.astype(F32), 0)
    dbias_term = jnp.sum(grad_mlp_own.astype(F32), 0)
    active_late = after(active, grad_branch_own)
    result = middle + column_scatter(active_late, down_local, 0, False) + dbias
    layer_out = jnp.where(live, result, 0.0).astype(BF)

    grad_branch = both_cores(plane_pieces(grad_branch_own))
    grad_attended = dot(grad_branch, proj_local, 1, 1).astype(BF)
    proj_grad = lax.psum_scatter(
        dot(attended, grad_branch, 0, 0).astype(BF), "fsdp", scatter_dimension=0, tiled=True
    ).astype(F32)
    grad_queries, grad_keys, grad_values = [], 0.0, 0.0
    for h in range(share):
        q, probs = heads[h]
        ga = grad_attended[:, h * HD : (h + 1) * HD]
        delta = jnp.sum(ga.astype(F32) * attended_f[h], -1, keepdims=True)
        grad_scores = (probs * (dot(ga, values, 1, 1) - delta)).astype(BF)
        grad_queries.append((dot(grad_scores, keys, 1, 0) * scale).astype(BF))
        grad_keys = grad_keys + dot(grad_scores, q, 0, 0)
        grad_values = grad_values + dot(probs.astype(BF), ga, 0, 0)
    grad_keys = grad_keys * scale
    given = jnp.where(core == 0, grad_values, grad_keys).astype(BF)
    given = jnp.roll(exchange(given, 1), total // 2, 0).astype(F32)
    grad_kind = (jnp.where(core == 0, grad_keys, grad_values) + given).astype(BF)
    grad_mixed = jnp.concatenate(grad_queries + [grad_kind], 1)
    grad_one = plane_scatter(grad_mixed, qkv_local, 1)
    qkv_term = dot(normed_one, grad_mixed, 0, 0).astype(BF)
    qkv_term = qkv_term.reshape(count, depth, wrows, wide_cols).transpose(1, 0, 2, 3)
    qkv_grad = lax.psum_scatter(
        qkv_term.reshape(depth * count * wrows, wide_cols),
        "fsdp",
        scatter_dimension=0,
        tiled=True,
    ).reshape(count, wrows, wide_cols)
    qkv_grad = lax.all_to_all(qkv_grad, "ctx", 0, 0, tiled=True).transpose(1, 0, 2).astype(F32)
    kinds = jnp.sum(qkv_grad[:, :, qcols:].reshape(wrows, chips, 2 * HD), 1)
    qkv_grad = jnp.concatenate([qkv_grad[:, :, :qcols].reshape(wrows, width), kinds], 1)
    scaled_one, inverse_one = normalize(own_rows)
    gain_one_term = jnp.sum(grad_one * scaled_one, 0)
    shift_one_term = jnp.sum(grad_one, 0)
    input_grad = grad_middle + norm_backward(grad_one, scaled_one, inverse_one, gain_one)

    up_grad = lax.all_to_all(
        up_grad.reshape(2 * depth, wrows, chips * frows),
        BOTH,
        0,
        0,
        tiled=True,
        axis_index_groups=chip_devices(),
    )
    up_grad = (
        up_grad.reshape(2 * depth, wrows, chips, frows)
        .transpose(1, 2, 0, 3)
        .reshape(wrows, hidden)
        .astype(F32)
    )
    down_grad = down_grad.astype(F32)

    mixed_term = jnp.sum(grad_mixed.astype(F32), 0)
    qbias_term = mixed_term[:qcols]
    vbias_term = jnp.where(core == 1, mixed_term[qcols:], 0.0)
    wide = [gain_one_term, shift_one_term, pbias_term, gain_two_term, shift_two_term, dbias_term]
    spread = jnp.concatenate(
        [v.reshape(count, depth, -1) for v in wide + [vbias_term]], 2
    ).reshape(count, -1)
    ub = ubias_term.reshape(chips, 1, frows) * (jnp.arange(2) == core).astype(F32)[None, :, None]
    spread = jnp.concatenate([spread, ub.reshape(count, frows)], 1)
    held = spread.shape[1]
    spread = jnp.pad(spread, ((0, 0), (0, -held % 1024))).reshape(count, -1, 128)
    first = jnp.sum(lax.all_to_all(spread, "ctx", 0, 0, tiled=True), 0).reshape(-1)
    ubias_grad = first[held - frows : held]
    second = jnp.concatenate(
        [first[: held - frows].reshape(depth, -1), qbias_term.reshape(depth, -1)], 1
    )
    kept = second.shape[1]
    second = jnp.pad(second, ((0, 0), (0, -kept % 1024))).reshape(depth, -1, 128)
    second = jnp.sum(lax.all_to_all(second, "fsdp", 0, 0, tiled=True), 0).reshape(-1)
    wide_grads = [second[i * wrows : (i + 1) * wrows] for i in range(6)]
    edge = 6 * wrows
    vn = value_bias.shape[0]
    vbias_grad = second[edge : edge + vn]
    qbias_grad = second[edge + vn : edge + vn + wrows]
    return (
        layer_out[None],
        input_grad[None],
        wide_grads[0],
        wide_grads[1],
        qkv_grad,
        qbias_grad,
        vbias_grad,
        proj_grad,
        wide_grads[2],
        wide_grads[3],
        wide_grads[4],
        up_grad,
        ubias_grad,
        down_grad,
        wide_grads[5],
    )


def solution(mesh):
    rows = P("fsdp", "ctx", None)
    vector = P(BOTH)
    matrix = P(BOTH, None)
    return jax.shard_map(
        body,
        mesh=mesh,
        in_specs=(
            rows, rows, P("fsdp"), vector, vector, matrix, vector, vector, matrix,
            vector, vector, vector, matrix, vector, matrix, vector,
        ),
        out_specs=(
            rows, rows, vector, vector, matrix, vector, vector, matrix, vector,
            vector, vector, matrix, vector, matrix, vector,
        ),
        check_vma=False,
    )
```

```python
import math

import jax
import jax.numpy as jnp
from jax import lax
from jax.experimental import pallas as pl
from jax.experimental.pallas import tpu as pltpu
from jax.sharding import PartitionSpec as P

HEADS = 16
HD = 128
EPS = 1e-05
NEG = -1e30
TILE = 256
BOTH = ("ctx", "fsdp")
BF = jnp.bfloat16
F32 = jnp.float32


def dot(a, b, da, db):
    return lax.dot_general(
        a, b, (((da,), (db,)), ((), ())), preferred_element_type=F32
    )


def normalize(values):
    center = values - jnp.mean(values, -1, keepdims=True)
    inverse = lax.rsqrt(jnp.mean(center * center, -1, keepdims=True) + EPS)
    return center * inverse, inverse


def norm_backward(grad, scaled, inverse, gain):
    inner = grad * gain
    return inverse * (
        inner
        - jnp.mean(inner, -1, keepdims=True)
        - scaled * jnp.mean(inner * scaled, -1, keepdims=True)
    )


def gelu(values):
    return jax.nn.gelu(values, approximate=True)


def attend_kernel(q_ref, k_ref, v_ref, row_limit_ref, key_pos_ref, out_ref):
    scale = 1.0 / math.sqrt(HD)
    allowed = key_pos_ref[...] <= row_limit_ref[...]
    scores = jnp.where(allowed, dot(q_ref[...], k_ref[...], 1, 1) * scale, NEG)
    top = jnp.max(scores, -1, keepdims=True)
    expo = jnp.exp(scores - top)
    probs = expo * (1.0 / jnp.sum(expo, -1, keepdims=True))
    out_ref[...] = dot(probs.astype(BF), v_ref[...], 1, 0).astype(BF)


def attend(queries, keys, values, limit, pos):
    rows = min(TILE, queries.shape[0])
    count = queries.shape[1] // HD
    tile = pl.BlockSpec((rows, HD), lambda h, i: (i, h))
    whole = pl.BlockSpec(keys.shape, lambda h, i: (0, 0))
    return pl.pallas_call(
        attend_kernel,
        grid=(count, queries.shape[0] // rows),
        in_specs=[
            tile,
            whole,
            whole,
            pl.BlockSpec((rows, 1), lambda h, i: (i, 0)),
            pl.BlockSpec((1, keys.shape[0]), lambda h, i: (0, 0)),
        ],
        out_specs=tile,
        out_shape=jax.ShapeDtypeStruct(queries.shape, BF),
        cost_estimate=pl.CostEstimate(flops=0, bytes_accessed=0, transcendentals=0),
        name="attend",
    )(queries, keys, values, limit[:, None], pos[None, :])


def attend_back_kernel(
    q_ref, k_ref, v_ref, grad_ref, row_limit_ref, key_pos_ref, gq_ref, gk_ref, gv_ref
):
    scale = 1.0 / math.sqrt(HD)

    @pl.when((pl.program_id(0) == 0) & (pl.program_id(1) == 0))
    def _():
        gk_ref[...] = jnp.zeros_like(gk_ref)
        gv_ref[...] = jnp.zeros_like(gv_ref)

    q, k, v, grad = q_ref[...], k_ref[...], v_ref[...], grad_ref[...]
    allowed = key_pos_ref[...] <= row_limit_ref[...]
    scores = jnp.where(allowed, dot(k, q, 1, 1) * scale, NEG)
    top = jnp.max(scores, 0, keepdims=True)
    expo = jnp.exp(scores - top)
    probs = expo * (1.0 / jnp.sum(expo, 0, keepdims=True))
    gv_ref[...] += dot(probs.astype(BF), grad, 1, 0)
    grad_probs = dot(v, grad, 1, 1)
    delta = jnp.sum(probs * grad_probs, 0, keepdims=True)
    grad_scores = (probs * (grad_probs - delta)).astype(BF)
    gk_ref[...] += dot(grad_scores, q, 1, 0) * scale
    gq_ref[...] = (dot(grad_scores, k, 0, 0) * scale).astype(BF)


def attend_back(queries, keys, values, grads, limit, pos):
    rows = min(TILE, queries.shape[0])
    count = queries.shape[1] // HD
    tile = pl.BlockSpec((rows, HD), lambda h, i: (i, h))
    whole = pl.BlockSpec(keys.shape, lambda h, i: (0, 0))
    return pl.pallas_call(
        attend_back_kernel,
        grid=(count, queries.shape[0] // rows),
        in_specs=[
            tile,
            whole,
            whole,
            tile,
            pl.BlockSpec((1, rows), lambda h, i: (0, i)),
            pl.BlockSpec((keys.shape[0], 1), lambda h, i: (0, 0)),
        ],
        out_specs=[tile, whole, whole],
        out_shape=[
            jax.ShapeDtypeStruct(queries.shape, BF),
            jax.ShapeDtypeStruct(keys.shape, F32),
            jax.ShapeDtypeStruct(keys.shape, F32),
        ],
        cost_estimate=pl.CostEstimate(flops=0, bytes_accessed=0, transcendentals=0),
        name="attend_back",
    )(queries, keys, values, grads, limit[None, :], pos[:, None])


def stage(*values):
    return lax.optimization_barrier(values)


def dot_over_rows(lefts, rights):
    return dot(lefts[0], rights[0], 0, 0) + dot(lefts[1], rights[1], 0, 0)


def exchange(value, mask):
    count = lax.axis_size("ctx")
    return lax.ppermute(value, "ctx", [(i, i ^ mask) for i in range(count)])


def chip_groups():
    count = lax.axis_size("ctx")
    return [list(range(core, count, 2)) for core in range(2)]


def chip_devices():
    width = 2 * lax.axis_size("fsdp")
    total = lax.axis_size("ctx") * lax.axis_size("fsdp")
    return [list(range(at, at + width)) for at in range(0, total, width)]


def plane_direct(value):
    chips = lax.axis_size("ctx") // 2
    return [value] + [exchange(value, 2 * k) for k in range(1, chips)]


def both_cores(own):
    return own, exchange(own, 1)


def core_sum(lefts, weight, dim):
    other, early = stage(dot(lefts[1], weight, 1, dim).astype(BF), lefts[0])
    return stage(dot(early, weight, 1, dim), exchange(other, 1))


def plane_parts(halves):
    own, other = halves
    chips = lax.axis_size("ctx") // 2
    rows = own.shape[0] // chips
    parts = [
        own[k * rows : (k + 1) * rows] + other[k * rows : (k + 1) * rows].astype(F32)
        for k in range(chips)
    ]
    return [parts[0]] + [piece.astype(BF) for piece in parts[1:]]


def plane_sum(parts, fill=None):
    chips = lax.axis_size("ctx") // 2
    arrived = [exchange(parts[k], 2 * k) for k in range(1, chips - 1)]
    filled = fill(*parts) if fill else ()
    last = stage(parts[chips - 1], filled)[0]
    total = parts[0]
    for piece in arrived + [exchange(last, 2 * chips - 2)]:
        total = total + piece.astype(F32)
    return total, filled


def turned(value, by):
    depth = lax.axis_size("fsdp")
    return lax.ppermute(value, "fsdp", [(i, (i + by) % depth) for i in range(depth)])


def slot(s):
    depth = lax.axis_size("fsdp")
    return (lax.axis_index("fsdp") - s) % depth


def near_rows(value):
    depth = lax.axis_size("fsdp")
    return {s: turned(value, s) for s in range(1, depth) if s != depth // 2}


def far_rows(value, near):
    depth = lax.axis_size("fsdp")
    pieces = {0: value, **near, depth // 2: turned(value, depth // 2)}
    rows = jnp.zeros((depth,) + value.shape, value.dtype)
    for s, piece in pieces.items():
        rows = lax.dynamic_update_slice(rows, piece[None], (slot(s), 0, 0))
    return rows.reshape(depth * value.shape[0], value.shape[1])


def column_parts(own, other=None):
    depth = lax.axis_size("fsdp")
    rows = own.shape[0] // depth
    parts = []
    for s in range(depth):
        part = lax.dynamic_slice_in_dim(own, slot(s) * rows, rows, 0)
        if other is not None:
            theirs = lax.dynamic_slice_in_dim(other, slot(s) * rows, rows, 0)
            part = part + theirs.astype(F32)
        parts.append(part.astype(BF) if s else part.astype(F32))
    return parts


def column_near(parts):
    depth = len(parts)
    return [parts[0]] + [turned(parts[s], -s) for s in range(1, depth) if s != depth // 2]


def column_far(parts, near):
    middle = len(parts) // 2
    total = turned(parts[middle], -middle).astype(F32)
    for piece in near:
        total = total + piece.astype(F32)
    return total


def lay_out(vectors, width):
    row, column, laid, places = 0, 0, 0, []
    for v in vectors:
        n = v.shape[0]
        if column + n > width:
            row, column = row + 1, 0
        places.append((row, column, n))
        laid = laid + jnp.pad(v[None], ((row, 7 - row), (column, width - column - n)))
        column += -(-n // 128) * 128
    return laid, places


def body(
    hidden_in,
    out_cotangent,
    seq_lengths,
    first_gain,
    first_shift,
    qkv_weight,
    query_bias,
    value_bias,
    proj_weight,
    proj_bias,
    second_gain,
    second_shift,
    up_weight,
    up_bias,
    down_weight,
    down_bias,
):
    count, depth = lax.axis_size("ctx"), lax.axis_size("fsdp")
    chips = count // 2
    at, level = lax.axis_index("ctx"), lax.axis_index("fsdp")
    core, chip = at % 2, at // 2
    span, width = hidden_in.shape[1:]
    wrows = qkv_weight.shape[0]
    hidden = up_weight.shape[1]
    frows = down_weight.shape[0]
    share = HEADS // count
    qcols = share * HD
    wide_cols = qcols + HD
    total = span * count
    length = seq_lengths[0]
    positions = at * span + jnp.arange(span, dtype=jnp.int32)
    live = (positions < length)[:, None]

    small = [
        first_gain,
        first_shift,
        query_bias,
        value_bias,
        proj_bias,
        second_gain,
        second_shift,
        up_bias,
        down_bias,
    ]
    packed, places = lay_out(small, wide_cols)
    qpart = qkv_weight[:, :width].reshape(wrows, count, qcols).transpose(1, 0, 2)
    kvpart = qkv_weight[:, width:].reshape(wrows, 2, HD).transpose(1, 0, 2)
    kvpart = jnp.broadcast_to(kvpart[None], (chips, 2, wrows, HD)).reshape(count, wrows, HD)
    outgoing = jnp.concatenate(
        [
            jnp.concatenate([qpart, kvpart], 2),
            jnp.broadcast_to(packed[None], (count,) + packed.shape),
        ],
        1,
    )
    incoming = lax.all_to_all(outgoing, "ctx", 0, 0, tiled=True)
    incoming, hidden_own, upstream = stage(incoming, hidden_in[0], out_cotangent[0])

    attn_all = lax.all_gather(incoming, "fsdp", axis=0)
    row_pieces = plane_direct(hidden_own)
    row_halves = both_cores(jnp.concatenate(row_pieces, 0))
    down_pieces = plane_direct(stage(down_weight, row_pieces)[0])
    own_rows = hidden_own.astype(F32)
    upstream = jnp.where(live, upstream.astype(F32), 0.0)
    grad_mlp_own = upstream.astype(BF)
    attn_all, row_halves, grad_mlp_own, proj_own, up_own = stage(
        attn_all, row_halves, grad_mlp_own, proj_weight, up_weight
    )

    proj_local = lax.all_gather(proj_own, "fsdp", axis=0, tiled=True)
    mlp_rows = lax.all_gather(grad_mlp_own, "fsdp", axis=0, tiled=True)
    up_parts = (
        up_own.reshape(wrows, chips, 2 * depth, frows)
        .transpose(2, 0, 1, 3)
        .reshape(2 * depth, wrows, chips * frows)
    )
    up_parts = lax.all_to_all(
        up_parts, BOTH, 0, 0, tiled=True, axis_index_groups=chip_devices()
    ).reshape(2 * depth * wrows, chips * frows)
    attn_rows = attn_all.transpose(1, 0, 2, 3)
    qkv_local = attn_rows[:, :, :wrows].reshape(width, wide_cols)
    table = attn_rows[:, :, wrows:].reshape(count * depth, 8, wide_cols)
    vectors = [table[:, r, c : c + n].reshape(-1).astype(F32) for r, c, n in places]
    gain_one, shift_one, qbias, vbias, pbias, gain_two, shift_two, ubias, dbias = vectors
    qbias = lax.dynamic_slice(qbias, (at * qcols,), (qcols,))
    ubias = lax.dynamic_slice(
        ubias.reshape(chips, 2 * depth, frows), (0, core * depth + level, 0), (chips, 1, frows)
    ).reshape(-1)
    normed_one = [
        (normalize(half.astype(F32))[0] * gain_one + shift_one).astype(BF) for half in row_halves
    ]
    mixed = jnp.concatenate([dot(half, qkv_local, 1, 0) for half in normed_one], 0)
    queries = (mixed[:, :qcols] + qbias).astype(BF)
    mine = (mixed[:, qcols:] + jnp.where(core == 1, vbias, 0.0)).astype(BF)
    theirs = jnp.roll(exchange(mine, 1), total // 2, 0)
    keys = jnp.where(core == 0, mine, theirs)
    values = jnp.where(core == 0, theirs, mine)
    base = jnp.stack([at ^ (2 * k + j) for j in range(2) for k in range(chips)]) * span
    pos = (base[:, None] + jnp.arange(span, dtype=jnp.int32)[None]).reshape(total)
    limit = jnp.minimum(pos, length - 1)
    attended = attend(queries, keys, values, limit, pos)
    held = (pbias, gain_two, shift_two, ubias, dbias)
    attended, up_parts, held, proj_local, down_pieces = stage(
        attended, up_parts, held, proj_local, down_pieces
    )
    pbias, gain_two, shift_two, ubias, dbias = held

    attended_halves = attended[: total // 2], attended[total // 2 :]
    down_local = jnp.zeros((chips, frows, width), BF)
    for k, piece in enumerate(down_pieces):
        down_local = lax.dynamic_update_slice(down_local, piece[None], (chip ^ k, 0, 0))
    down_local = down_local.reshape(chips * frows, width)
    branch, _ = plane_sum(plane_parts(core_sum(attended_halves, proj_local, 0)))
    middle = own_rows + branch + pbias
    scaled_two, inverse_two = normalize(middle)
    normed_two_own = (scaled_two * gain_two + shift_two).astype(BF)
    normed_two_own, down_local = stage(normed_two_own, down_local)

    up_local = lax.all_gather(
        stage(up_parts, mlp_rows)[0], "ctx", axis=0, tiled=True, axis_index_groups=chip_groups()
    )

    near = near_rows(normed_two_own)
    near, normed_value = stage(near, normed_two_own)
    mlp_halves = both_cores(stage(mlp_rows, near)[0])
    grad_active = [dot(half, down_local, 1, 1) for half in mlp_halves]
    normed_rows = far_rows(normed_value, near)
    normed_rows, mlp_halves, grad_active = stage(normed_rows, mlp_halves, grad_active)

    normed_halves = both_cores(normed_rows)
    active, grad_before = [], []
    befores = stage(*[dot(half, up_local, 1, 0) for half in normed_halves])
    for before, grad_half in zip(befores, grad_active):
        before = before + ubias
        active_f, gelu_pull = jax.vjp(gelu, before)
        active.append(active_f.astype(BF))
        grad_before.append(gelu_pull(grad_half)[0].astype(BF))

    def chip_sum(term):
        return lax.psum_scatter(
            term, "ctx", scatter_dimension=0, tiled=True, axis_index_groups=chip_groups()
        )

    two_parts = column_parts(*core_sum(grad_before, up_local, 1))

    held = stage(normed_halves, grad_before, active, mlp_halves, two_parts)
    normed, grads, acts, mlps = held[:4]
    up_term = dot_over_rows(normed, grads).astype(BF)
    down_term = dot_over_rows(acts, mlps).astype(BF)
    ubias_term = jnp.sum(grads[0].astype(F32), 0) + jnp.sum(grads[1].astype(F32), 0)
    near, two_parts, up_term, down_term, ubias_term = stage(
        column_near(two_parts), two_parts, up_term, down_term, ubias_term
    )
    up_grad = chip_sum(up_term)
    out_own, out_other = core_sum(stage(acts, near)[0], down_local, 0)
    out_term = (out_own + out_other.astype(F32)).astype(BF)
    grad_two = column_far(two_parts, near)
    gain_two_term = jnp.sum(grad_two * scaled_two, 0)
    shift_two_term = jnp.sum(grad_two, 0)
    grad_middle = upstream + norm_backward(grad_two, scaled_two, inverse_two, gain_two)
    grad_branch_own = grad_middle.astype(BF)
    grad_branch_own, out_term, down_term = stage(grad_branch_own, out_term, down_term)

    branch_halves = both_cores(jnp.concatenate(plane_direct(grad_branch_own), 0))
    pbias_term = jnp.sum(grad_branch_own.astype(F32), 0)
    dbias_term = jnp.sum(grad_mlp_own.astype(F32), 0)
    out_sum = lax.psum_scatter(out_term, "fsdp", scatter_dimension=0, tiled=True)
    branch_halves, pbias_term, dbias_term, down_term, up_grad = stage(
        branch_halves, pbias_term, dbias_term, down_term, up_grad
    )

    grad_attended = jnp.concatenate(
        [dot(half, proj_local, 1, 1) for half in branch_halves], 0
    ).astype(BF)
    grad_queries, grad_keys, grad_values = attend_back(
        queries, keys, values, grad_attended, limit, pos
    )
    given = jnp.where(core == 0, grad_values, grad_keys).astype(BF)
    given = jnp.roll(exchange(given, 1), total // 2, 0).astype(F32)
    grad_kind = (jnp.where(core == 0, grad_keys, grad_values) + given).astype(BF)
    grad_mixed = jnp.concatenate([grad_queries, grad_kind], 1)
    up_grad = lax.all_to_all(
        up_grad.reshape(2 * depth, wrows, chips * frows),
        BOTH,
        0,
        0,
        tiled=True,
        axis_index_groups=chip_devices(),
    )
    grad_mixed, up_grad = stage(grad_mixed, up_grad)

    mixed_halves = grad_mixed[: total // 2], grad_mixed[total // 2 :]
    proj_term = dot_over_rows(attended_halves, branch_halves).astype(BF)
    one_sums = core_sum(mixed_halves, qkv_local, 1)
    one_sums, proj_term, out_sum = stage(one_sums, proj_term, out_sum)
    proj_grad = lax.psum_scatter(proj_term, "fsdp", scatter_dimension=0, tiled=True)
    down_grad = chip_sum(stage(down_term, proj_term)[0])
    one_parts = plane_parts(one_sums)

    def qkv_parts(*gate):
        halves = stage(mixed_halves, gate)[0]
        term = dot_over_rows(normed_one, halves).astype(BF)
        term = term.reshape(count, depth, wrows, wide_cols).transpose(1, 0, 2, 3)
        return column_parts(term.reshape(depth * count * wrows, wide_cols))

    grad_one, qkv_term = plane_sum(one_parts, qkv_parts)
    qkv_near = column_near(qkv_term)
    scaled_one, inverse_one = normalize(own_rows)
    gain_one_term = jnp.sum(grad_one * scaled_one, 0)
    shift_one_term = jnp.sum(grad_one, 0)
    held = (grad_one, qkv_term, qkv_near, up_grad)
    gain_one_term, shift_one_term, held = stage(gain_one_term, shift_one_term, held)
    grad_one, qkv_term, qkv_near, up_grad = held

    result = middle + out_sum.astype(F32) + dbias
    layer_out = jnp.where(live, result, 0.0).astype(BF)
    qkv_grad = column_far(qkv_term, qkv_near).astype(BF)
    qkv_grad = qkv_grad.reshape(count, wrows, wide_cols)
    input_grad = grad_middle + norm_backward(grad_one, scaled_one, inverse_one, gain_one)
    up_grad = (
        up_grad.reshape(2 * depth, wrows, chips, frows)
        .transpose(1, 2, 0, 3)
        .reshape(wrows, hidden)
        .astype(F32)
    )
    qkv_grad = lax.all_to_all(qkv_grad, "ctx", 0, 0, tiled=True).transpose(1, 0, 2).astype(F32)
    kinds = jnp.sum(qkv_grad[:, :, qcols:].reshape(wrows, chips, 2 * HD), 1)
    qkv_grad = jnp.concatenate([qkv_grad[:, :, :qcols].reshape(wrows, width), kinds], 1)
    down_grad = down_grad.astype(F32)
    proj_grad = proj_grad.astype(F32)

    mixed_term = jnp.sum(grad_mixed.astype(F32), 0)
    vbias_term = jnp.where(core == 1, mixed_term[qcols:], 0.0).reshape(count * depth, -1)
    vbias_term = jnp.pad(vbias_term, ((0, 0), (0, wrows - vbias_term.shape[1]))).reshape(-1)
    ubias_term = ubias_term.reshape(chips, 1, frows)
    ubias_term = jnp.where(jnp.arange(2)[None, :, None] == core, ubias_term, 0.0)
    terms = [pbias_term, gain_two_term, shift_two_term, dbias_term, vbias_term]
    early = jnp.stack(terms + [jnp.zeros_like(vbias_term)] * 3)
    early = early.reshape(8, count, -1)
    ub = jnp.pad(ubias_term.reshape(1, count, frows), ((0, 7), (0, 0), (0, 0)))
    early, ub = early.transpose(1, 0, 2), ub.transpose(1, 0, 2)
    late = jnp.stack([gain_one_term, shift_one_term]).reshape(2, count, -1).transpose(1, 0, 2)
    late = jnp.pad(late, ((0, 0), (5, 1), (0, 0)))
    block = late.shape[2]
    first = lax.all_to_all(
        jnp.concatenate([early + late, ub], 2), "ctx", 0, 0, tiled=True
    )
    first = jnp.sum(first, 0)
    ubias_grad = first[0, block:]
    second = first[:, :block] + jnp.pad(mixed_term[None, :qcols], ((7, 0), (0, 0)))
    second = second.reshape(8, depth, wrows).transpose(1, 0, 2)
    second = jnp.sum(lax.all_to_all(second, "fsdp", 0, 0, tiled=True), 0)
    wide_grads = [second[i] for i in (5, 6, 0, 1, 2, 3)]
    vbias_grad = second[4, : value_bias.shape[0]]
    qbias_grad = second[7]
    return (
        layer_out[None],
        input_grad[None],
        wide_grads[0],
        wide_grads[1],
        qkv_grad,
        qbias_grad,
        vbias_grad,
        proj_grad,
        wide_grads[2],
        wide_grads[3],
        wide_grads[4],
        up_grad,
        ubias_grad,
        down_grad,
        wide_grads[5],
    )


def solution(mesh):
    rows = P("fsdp", "ctx", None)
    vector = P(BOTH)
    matrix = P(BOTH, None)
    return jax.shard_map(
        body,
        mesh=mesh,
        in_specs=(
            rows, rows, P("fsdp"), vector, vector, matrix, vector, vector, matrix,
            vector, vector, vector, matrix, vector, matrix, vector,
        ),
        out_specs=(
            rows, rows, vector, vector, matrix, vector, vector, matrix, vector,
            vector, vector, matrix, vector, matrix, vector,
        ),
        check_vma=False,
    )
```

```python
import functools
import math

import jax
import jax.numpy as jnp
from jax import lax
from jax.experimental import pallas as pl
from jax.experimental.pallas import tpu as pltpu
from jax.sharding import PartitionSpec as P

HEADS = 16
HD = 128
EPS = 1e-05
NEG = -1e30
TILE = 256
BOTH = ("ctx", "fsdp")
BF = jnp.bfloat16
F32 = jnp.float32


def dot(a, b, da, db):
    return lax.dot_general(
        a, b, (((da,), (db,)), ((), ())), preferred_element_type=F32
    )


def normalize(values):
    center = values - jnp.mean(values, -1, keepdims=True)
    inverse = lax.rsqrt(jnp.mean(center * center, -1, keepdims=True) + EPS)
    return center * inverse, inverse


def norm_backward(grad, scaled, inverse, gain):
    inner = grad * gain
    return inverse * (
        inner
        - jnp.mean(inner, -1, keepdims=True)
        - scaled * jnp.mean(inner * scaled, -1, keepdims=True)
    )


def gelu(values):
    return jax.nn.gelu(values, approximate=True)


def attend_kernel(q_ref, k_ref, v_ref, row_limit_ref, key_pos_ref, out_ref):
    scale = 1.0 / math.sqrt(HD)
    allowed = key_pos_ref[...] <= row_limit_ref[...]
    scores = jnp.where(allowed, dot(q_ref[...], k_ref[...], 1, 1) * scale, NEG)
    top = jnp.max(scores, -1, keepdims=True)
    expo = jnp.exp(scores - top)
    probs = expo * (1.0 / jnp.sum(expo, -1, keepdims=True))
    out_ref[...] = dot(probs.astype(BF), v_ref[...], 1, 0).astype(BF)


def attend(queries, keys, values, limit, pos):
    rows = min(TILE, queries.shape[0])
    count = queries.shape[1] // HD - 1
    tile = pl.BlockSpec((rows, HD), lambda h, i: (i, h))
    whole = pl.BlockSpec(keys.shape, lambda h, i: (0, 0))
    return pl.pallas_call(
        attend_kernel,
        grid=(count, queries.shape[0] // rows),
        in_specs=[
            tile,
            whole,
            whole,
            pl.BlockSpec((rows, 1), lambda h, i: (i, 0)),
            pl.BlockSpec((1, keys.shape[0]), lambda h, i: (0, 0)),
        ],
        out_specs=tile,
        out_shape=jax.ShapeDtypeStruct((queries.shape[0], count * HD), BF),
        cost_estimate=pl.CostEstimate(flops=0, bytes_accessed=0, transcendentals=0),
        name="attend",
    )(queries, keys, values, limit[:, None], pos[None, :])


def attend_back_kernel(
    q_ref, k_ref, v_ref, grad_ref, row_limit_ref, key_pos_ref, gq_ref, gk_ref, gv_ref
):
    scale = 1.0 / math.sqrt(HD)

    @pl.when((pl.program_id(0) == 0) & (pl.program_id(1) == 0))
    def _():
        gk_ref[...] = jnp.zeros_like(gk_ref)
        gv_ref[...] = jnp.zeros_like(gv_ref)

    q, k, v, grad = q_ref[...], k_ref[...], v_ref[...], grad_ref[...]
    allowed = key_pos_ref[...] <= row_limit_ref[...]
    scores = jnp.where(allowed, dot(k, q, 1, 1) * scale, NEG)
    top = jnp.max(scores, 0, keepdims=True)
    expo = jnp.exp(scores - top)
    probs = expo * (1.0 / jnp.sum(expo, 0, keepdims=True))
    gv_ref[...] += dot(probs.astype(BF), grad, 1, 0)
    grad_probs = dot(v, grad, 1, 1)
    delta = jnp.sum(probs * grad_probs, 0, keepdims=True)
    grad_scores = (probs * (grad_probs - delta)).astype(BF)
    gk_ref[...] += dot(grad_scores, q, 1, 0) * scale
    gq_ref[...] = (dot(grad_scores, k, 0, 0) * scale).astype(BF)


def attend_back(queries, keys, values, grads, limit, pos):
    rows = min(TILE, queries.shape[0])
    count = queries.shape[1] // HD - 1
    tile = pl.BlockSpec((rows, HD), lambda h, i: (i, h))
    whole = pl.BlockSpec(keys.shape, lambda h, i: (0, 0))
    return pl.pallas_call(
        attend_back_kernel,
        grid=(count, queries.shape[0] // rows),
        in_specs=[
            tile,
            whole,
            whole,
            tile,
            pl.BlockSpec((1, rows), lambda h, i: (0, i)),
            pl.BlockSpec((keys.shape[0], 1), lambda h, i: (0, 0)),
        ],
        out_specs=[tile, whole, whole],
        out_shape=[
            jax.ShapeDtypeStruct((queries.shape[0], count * HD), BF),
            jax.ShapeDtypeStruct(keys.shape, F32),
            jax.ShapeDtypeStruct(keys.shape, F32),
        ],
        cost_estimate=pl.CostEstimate(flops=0, bytes_accessed=0, transcendentals=0),
        name="attend_back",
    )(queries, keys, values, grads, limit[None, :], pos[:, None])


def stage(*values):
    return lax.optimization_barrier(values)


def call(kernel, grid, in_specs, out_specs, out_shape, name):
    return pl.pallas_call(
        kernel,
        grid=grid,
        in_specs=in_specs,
        out_specs=out_specs,
        out_shape=out_shape,
        cost_estimate=pl.CostEstimate(flops=0, bytes_accessed=0, transcendentals=0),
        name=name,
    )


def multiply_kernel(dim, a_ref, b_ref, out_ref):
    out_ref[...] = dot(a_ref[...], b_ref[...], 1, dim).astype(out_ref.dtype)


def multiply(a, b, dim, dtype=F32):
    rows, depth = a.shape
    columns = b.shape[1 - dim]
    tile = min(512, columns)
    if dim:
        b_spec = pl.BlockSpec((tile, depth), lambda j: (j, 0))
    else:
        b_spec = pl.BlockSpec((depth, tile), lambda j: (0, j))
    return call(
        functools.partial(multiply_kernel, dim),
        (columns // tile,),
        [pl.BlockSpec((rows, depth), lambda j: (0, 0)), b_spec],
        pl.BlockSpec((rows, tile), lambda j: (0, j)),
        jax.ShapeDtypeStruct((rows, columns), dtype),
        "multiply",
    )(a, b)


def over_rows_kernel(a0_ref, a1_ref, b0_ref, b1_ref, out_ref):
    total = dot(a0_ref[...], b0_ref[...], 0, 0) + dot(a1_ref[...], b1_ref[...], 0, 0)
    out_ref[...] = total.astype(BF)


def dot_over_rows(lefts, rights):
    rows, height = lefts[0].shape
    width = rights[0].shape[1]
    tile = min(256, height)
    left = pl.BlockSpec((rows, tile), lambda i: (0, i))
    right = pl.BlockSpec((rows, width), lambda i: (0, 0))
    return call(
        over_rows_kernel,
        (height // tile,),
        [left, left, right, right],
        pl.BlockSpec((tile, width), lambda i: (i, 0)),
        jax.ShapeDtypeStruct((height, width), BF),
        "over_rows",
    )(*lefts, *rights)


def plain_over_rows(lefts, rights):
    return (dot(lefts[0], rights[0], 0, 0) + dot(lefts[1], rights[1], 0, 0)).astype(BF)


def hidden_kernel(x0_ref, x1_ref, w_ref, bias_ref, g0_ref, g1_ref, a0_ref, a1_ref, o0_ref, o1_ref):
    root, cubic = math.sqrt(2.0 / math.pi), 0.044715
    halves = (x0_ref, g0_ref, a0_ref, o0_ref), (x1_ref, g1_ref, a1_ref, o1_ref)
    for x_ref, grad_ref, active_ref, out_ref in halves:
        u = dot(x_ref[...], w_ref[...], 1, 0) + bias_ref[...]
        square = u * u
        t = jnp.tanh(root * u * (1.0 + cubic * square))
        active_ref[...] = (0.5 * u * (1.0 + t)).astype(BF)
        slope = 0.5 * (1.0 + t) + 0.5 * u * (1.0 - t * t) * (root * (1.0 + 3.0 * cubic * square))
        out_ref[...] = (grad_ref[...] * slope).astype(BF)


def hidden_layer(halves, weight, bias, grads):
    count, width = halves[0].shape
    columns = weight.shape[1]
    tile = min(256, columns)
    whole = pl.BlockSpec((count, width), lambda j: (0, 0))
    piece = pl.BlockSpec((count, tile), lambda j: (0, j))
    a0, a1, o0, o1 = call(
        hidden_kernel,
        (columns // tile,),
        [
            whole,
            whole,
            pl.BlockSpec((width, tile), lambda j: (0, j)),
            pl.BlockSpec((1, tile), lambda j: (0, j)),
            piece,
            piece,
        ],
        [piece] * 4,
        [jax.ShapeDtypeStruct((count, columns), BF)] * 4,
        "hidden_layer",
    )(*halves, weight, bias[None], *grads)
    return (a0, a1), (o0, o1)


def exchange(value, mask):
    count = lax.axis_size("ctx")
    return lax.ppermute(value, "ctx", [(i, i ^ mask) for i in range(count)])


def chip_groups():
    count = lax.axis_size("ctx")
    return [list(range(core, count, 2)) for core in range(2)]


def chip_devices():
    width = 2 * lax.axis_size("fsdp")
    total = lax.axis_size("ctx") * lax.axis_size("fsdp")
    return [list(range(at, at + width)) for at in range(0, total, width)]


def plane_direct(value):
    chips = lax.axis_size("ctx") // 2
    return [value] + [exchange(value, 2 * k) for k in range(1, chips)]


def both_cores(own):
    return own, exchange(own, 1)


def core_sum(lefts, weight, dim):
    other, early = stage(dot(lefts[1], weight, 1, dim).astype(BF), lefts[0])
    return stage(dot(early, weight, 1, dim), exchange(other, 1))


def plane_parts(halves):
    own, other = halves
    chips = lax.axis_size("ctx") // 2
    rows = own.shape[0] // chips
    parts = [
        own[k * rows : (k + 1) * rows] + other[k * rows : (k + 1) * rows].astype(F32)
        for k in range(chips)
    ]
    return [parts[0]] + [piece.astype(BF) for piece in parts[1:]]


def plane_sum(parts, fill=None):
    chips = lax.axis_size("ctx") // 2
    arrived = [exchange(parts[k], 2 * k) for k in range(1, chips - 1)]
    filled = fill(*parts) if fill else ()
    last = stage(parts[chips - 1], filled)[0]
    total = parts[0]
    for piece in arrived + [exchange(last, 2 * chips - 2)]:
        total = total + piece.astype(F32)
    return total, filled


def turned(value, by):
    depth = lax.axis_size("fsdp")
    return lax.ppermute(value, "fsdp", [(i, (i + by) % depth) for i in range(depth)])


def slot(s):
    depth = lax.axis_size("fsdp")
    return (lax.axis_index("fsdp") - s) % depth


def near_rows(value):
    depth = lax.axis_size("fsdp")
    return {s: turned(value, s) for s in range(1, depth) if s != depth // 2}


def far_rows(value, near):
    depth = lax.axis_size("fsdp")
    pieces = {0: value, **near, depth // 2: turned(value, depth // 2)}
    rows = jnp.zeros((depth,) + value.shape, value.dtype)
    for s, piece in pieces.items():
        rows = lax.dynamic_update_slice(rows, piece[None], (slot(s), 0, 0))
    return rows.reshape(depth * value.shape[0], value.shape[1])


def column_parts(own, other=None):
    depth = lax.axis_size("fsdp")
    rows = own.shape[0] // depth
    parts = []
    for s in range(depth):
        part = lax.dynamic_slice_in_dim(own, slot(s) * rows, rows, 0)
        if other is not None:
            theirs = lax.dynamic_slice_in_dim(other, slot(s) * rows, rows, 0)
            part = part + theirs.astype(F32)
        parts.append(part.astype(BF) if s else part.astype(F32))
    return parts


def column_near(parts):
    depth = len(parts)
    return [parts[0]] + [turned(parts[s], -s) for s in range(1, depth) if s != depth // 2]


def column_far(parts, near):
    middle = len(parts) // 2
    total = turned(parts[middle], -middle).astype(F32)
    for piece in near:
        total = total + piece.astype(F32)
    return total


def lay_out(vectors, width):
    row, column, laid, places = 0, 0, 0, []
    for v in vectors:
        n = v.shape[0]
        if column + n > width:
            row, column = row + 1, 0
        places.append((row, column, n))
        laid = laid + jnp.pad(v[None], ((row, 7 - row), (column, width - column - n)))
        column += -(-n // 128) * 128
    return laid, places


def body(
    hidden_in,
    out_cotangent,
    seq_lengths,
    first_gain,
    first_shift,
    qkv_weight,
    query_bias,
    value_bias,
    proj_weight,
    proj_bias,
    second_gain,
    second_shift,
    up_weight,
    up_bias,
    down_weight,
    down_bias,
):
    count, depth = lax.axis_size("ctx"), lax.axis_size("fsdp")
    chips = count // 2
    at, level = lax.axis_index("ctx"), lax.axis_index("fsdp")
    core, chip = at % 2, at // 2
    span, width = hidden_in.shape[1:]
    wrows = qkv_weight.shape[0]
    hidden = up_weight.shape[1]
    frows = down_weight.shape[0]
    share = HEADS // count
    qcols = share * HD
    wide_cols = qcols + HD
    total = span * count
    length = seq_lengths[0]
    positions = at * span + jnp.arange(span, dtype=jnp.int32)
    live = (positions < length)[:, None]

    small = [
        first_gain,
        first_shift,
        query_bias,
        value_bias,
        proj_bias,
        second_gain,
        second_shift,
        up_bias,
        down_bias,
    ]
    packed, places = lay_out(small, wide_cols)
    qpart = qkv_weight[:, :width].reshape(wrows, count, qcols).transpose(1, 0, 2)
    kvpart = qkv_weight[:, width:].reshape(wrows, 2, HD).transpose(1, 0, 2)
    kvpart = jnp.broadcast_to(kvpart[None], (chips, 2, wrows, HD)).reshape(count, wrows, HD)
    outgoing = jnp.concatenate(
        [
            jnp.concatenate([qpart, kvpart], 2),
            jnp.broadcast_to(packed[None], (count,) + packed.shape),
        ],
        1,
    )
    incoming = lax.all_to_all(outgoing, "ctx", 0, 0, tiled=True)
    incoming, hidden_own, upstream = stage(incoming, hidden_in[0], out_cotangent[0])

    attn_all = lax.all_gather(incoming, "fsdp", axis=0)
    row_pieces = plane_direct(hidden_own)
    row_halves = both_cores(jnp.concatenate(row_pieces, 0))
    down_pieces = plane_direct(stage(down_weight, row_pieces)[0])
    own_rows = hidden_own.astype(F32)
    upstream = jnp.where(live, upstream.astype(F32), 0.0)
    grad_mlp_own = upstream.astype(BF)
    attn_all, row_halves, grad_mlp_own, proj_own, up_own = stage(
        attn_all, row_halves, grad_mlp_own, proj_weight, up_weight
    )

    proj_local = lax.all_gather(proj_own, "fsdp", axis=0, tiled=True)
    mlp_rows = lax.all_gather(grad_mlp_own, "fsdp", axis=0, tiled=True)
    up_parts = (
        up_own.reshape(wrows, chips, 2 * depth, frows)
        .transpose(2, 0, 1, 3)
        .reshape(2 * depth, wrows, chips * frows)
    )
    up_parts = lax.all_to_all(
        up_parts, BOTH, 0, 0, tiled=True, axis_index_groups=chip_devices()
    ).reshape(2 * depth * wrows, chips * frows)
    attn_rows = attn_all.transpose(1, 0, 2, 3)
    qkv_local = attn_rows[:, :, :wrows].reshape(width, wide_cols)
    table = attn_rows[:, :, wrows:].reshape(count * depth, 8, wide_cols)
    vectors = [table[:, r, c : c + n].reshape(-1).astype(F32) for r, c, n in places]
    gain_one, shift_one, qbias, vbias, pbias, gain_two, shift_two, ubias, dbias = vectors
    ubias = lax.dynamic_slice(
        ubias.reshape(chips, 2 * depth, frows), (0, core * depth + level, 0), (chips, 1, frows)
    ).reshape(-1)
    bias_one = jnp.concatenate(
        [
            lax.dynamic_slice(qbias, (at * qcols,), (qcols,)),
            jnp.where(core == 1, vbias, 0.0),
        ]
    )
    normed_one = [
        (normalize(half.astype(F32))[0] * gain_one + shift_one).astype(BF) for half in row_halves
    ]
    mixed = jnp.concatenate([dot(half, qkv_local, 1, 0) for half in normed_one], 0)
    queries = (mixed + bias_one).astype(BF)
    mine = queries[:, qcols:]
    theirs = jnp.roll(exchange(mine, 1), total // 2, 0)
    keys = jnp.where(core == 0, mine, theirs)
    values = jnp.where(core == 0, theirs, mine)
    base = jnp.stack([at ^ (2 * k + j) for j in range(2) for k in range(chips)]) * span
    pos = (base[:, None] + jnp.arange(span, dtype=jnp.int32)[None]).reshape(total)
    limit = jnp.minimum(pos, length - 1)
    attended = attend(queries, keys, values, limit, pos)
    held = (pbias, gain_two, shift_two, ubias, dbias)
    attended, up_parts, held, proj_local, down_pieces = stage(
        attended, up_parts, held, proj_local, down_pieces
    )
    pbias, gain_two, shift_two, ubias, dbias = held

    attended_halves = attended[: total // 2], attended[total // 2 :]
    down_local = jnp.zeros((chips, frows, width), BF)
    for k, piece in enumerate(down_pieces):
        down_local = lax.dynamic_update_slice(down_local, piece[None], (chip ^ k, 0, 0))
    down_local = down_local.reshape(chips * frows, width)
    branch, _ = plane_sum(plane_parts(core_sum(attended_halves, proj_local, 0)))
    middle = own_rows + branch + pbias
    scaled_two, inverse_two = normalize(middle)
    normed_two_own = (scaled_two * gain_two + shift_two).astype(BF)
    normed_two_own, down_local, up_parts, mlp_rows = stage(
        normed_two_own, down_local, up_parts, mlp_rows
    )

    up_local = lax.all_gather(
        up_parts, "ctx", axis=0, tiled=True, axis_index_groups=chip_groups()
    )

    near = near_rows(normed_two_own)
    mlp_halves = both_cores(mlp_rows)
    grad_active = [multiply(half, down_local, 1) for half in mlp_halves]
    near, normed_value, mlp_halves, grad_active = stage(
        near, normed_two_own, mlp_halves, grad_active
    )
    normed_rows = far_rows(normed_value, near)
    normed_rows = stage(normed_rows)[0]

    normed_halves = both_cores(normed_rows)
    active, grad_before = hidden_layer(normed_halves, up_local, ubias, grad_active)

    def chip_sum(term):
        return lax.psum_scatter(
            term, "ctx", scatter_dimension=0, tiled=True, axis_index_groups=chip_groups()
        )

    two_parts = column_parts(*core_sum(grad_before, up_local, 1))

    held = stage(normed_halves, grad_before, active, mlp_halves, two_parts)
    normed, grads, acts, mlps = held[:4]
    out_other = exchange(multiply(acts[1], down_local, 0, BF), 1)
    out_own = multiply(acts[0], down_local, 0)
    up_term = dot_over_rows(normed, grads)
    near, two_parts, up_term, out_own, out_other = stage(
        column_near(two_parts), two_parts, up_term, out_own, out_other
    )
    out_term = (out_own + out_other.astype(F32)).astype(BF)
    up_grad = chip_sum(up_term)
    acts, mlps, grads = stage(acts, mlps, grads, near)[:3]
    down_term = dot_over_rows(acts, mlps)
    ubias_term = jnp.sum(grads[0].astype(F32), 0) + jnp.sum(grads[1].astype(F32), 0)
    grad_two = column_far(two_parts, near)
    gain_two_term = jnp.sum(grad_two * scaled_two, 0)
    shift_two_term = jnp.sum(grad_two, 0)
    grad_middle = upstream + norm_backward(grad_two, scaled_two, inverse_two, gain_two)
    grad_branch_own = grad_middle.astype(BF)
    grad_branch_own, out_term, down_term, ubias_term = stage(
        grad_branch_own, out_term, down_term, ubias_term
    )
    out_sum = lax.psum_scatter(out_term, "fsdp", scatter_dimension=0, tiled=True)

    branch_halves = both_cores(jnp.concatenate(plane_direct(grad_branch_own), 0))
    pbias_term = jnp.sum(grad_branch_own.astype(F32), 0)
    dbias_term = jnp.sum(grad_mlp_own.astype(F32), 0)
    branch_halves, pbias_term, dbias_term, up_grad = stage(
        branch_halves, pbias_term, dbias_term, up_grad
    )

    grad_attended = jnp.concatenate(
        [dot(half, proj_local, 1, 1) for half in branch_halves], 0
    ).astype(BF)
    grad_queries, grad_keys, grad_values = attend_back(
        queries, keys, values, grad_attended, limit, pos
    )
    given = jnp.where(core == 0, grad_values, grad_keys).astype(BF)
    given = jnp.roll(exchange(given, 1), total // 2, 0).astype(F32)
    grad_kind = (jnp.where(core == 0, grad_keys, grad_values) + given).astype(BF)
    grad_mixed = jnp.concatenate([grad_queries, grad_kind], 1)

    grad_mixed, down_term = stage(grad_mixed, down_term)
    down_grad = chip_sum(down_term)

    mixed_halves = grad_mixed[: total // 2], grad_mixed[total // 2 :]
    proj_term = plain_over_rows(attended_halves, branch_halves)
    one_sums = core_sum(mixed_halves, qkv_local, 1)
    one_sums, proj_term, out_sum = stage(one_sums, proj_term, out_sum)
    one_parts = plane_parts(one_sums)
    up_grad = stage(up_grad, one_parts)[0]
    up_grad = lax.all_to_all(
        up_grad.reshape(2 * depth, wrows, chips * frows),
        BOTH,
        0,
        0,
        tiled=True,
        axis_index_groups=chip_devices(),
    )

    def qkv_parts(*gate):
        halves = stage(mixed_halves, gate)[0]
        term = plain_over_rows(normed_one, halves)
        term = term.reshape(count, depth, wrows, wide_cols).transpose(1, 0, 2, 3)
        return column_parts(term.reshape(depth * count * wrows, wide_cols))

    grad_one, qkv_term = plane_sum(one_parts, qkv_parts)
    qkv_near = column_near(qkv_term)
    scaled_one, inverse_one = normalize(own_rows)
    gain_one_term = jnp.sum(grad_one * scaled_one, 0)
    shift_one_term = jnp.sum(grad_one, 0)
    held = (grad_one, qkv_term, qkv_near, up_grad, proj_term)
    gain_one_term, shift_one_term, held = stage(gain_one_term, shift_one_term, held)
    grad_one, qkv_term, qkv_near, up_grad, proj_term = held

    result = middle + out_sum.astype(F32) + dbias
    layer_out = jnp.where(live, result, 0.0).astype(BF)
    qkv_grad = column_far(qkv_term, qkv_near).astype(BF)
    qkv_grad = qkv_grad.reshape(count, wrows, wide_cols)
    input_grad = grad_middle + norm_backward(grad_one, scaled_one, inverse_one, gain_one)
    up_grad = (
        up_grad.reshape(2 * depth, wrows, chips, frows)
        .transpose(1, 2, 0, 3)
        .reshape(wrows, hidden)
        .astype(F32)
    )
    qkv_grad = lax.all_to_all(qkv_grad, "ctx", 0, 0, tiled=True).transpose(1, 0, 2).astype(F32)
    kinds = jnp.sum(qkv_grad[:, :, qcols:].reshape(wrows, chips, 2 * HD), 1)
    qkv_grad = jnp.concatenate([qkv_grad[:, :, :qcols].reshape(wrows, width), kinds], 1)

    mixed_term = jnp.sum(grad_mixed.astype(F32), 0)
    vbias_term = jnp.where(core == 1, mixed_term[qcols:], 0.0).reshape(count * depth, -1)
    vbias_term = jnp.pad(vbias_term, ((0, 0), (0, wrows - vbias_term.shape[1]))).reshape(-1)
    ubias_term = ubias_term.reshape(chips, 1, frows)
    ubias_term = jnp.where(jnp.arange(2)[None, :, None] == core, ubias_term, 0.0)
    terms = [pbias_term, gain_two_term, shift_two_term, dbias_term, vbias_term]
    early = jnp.stack(terms + [jnp.zeros_like(vbias_term)] * 3)
    early = early.reshape(8, count, -1)
    ub = jnp.pad(ubias_term.reshape(1, count, frows), ((0, 7), (0, 0), (0, 0)))
    early, ub = early.transpose(1, 0, 2), ub.transpose(1, 0, 2)
    late = jnp.stack([gain_one_term, shift_one_term]).reshape(2, count, -1).transpose(1, 0, 2)
    late = jnp.pad(late, ((0, 0), (5, 1), (0, 0)))
    block = late.shape[2]
    first = lax.all_to_all(
        jnp.concatenate([early + late, ub], 2), "ctx", 0, 0, tiled=True
    )
    first = jnp.sum(first, 0)
    ubias_grad = first[0, block:]
    second = first[:, :block] + jnp.pad(mixed_term[None, :qcols], ((7, 0), (0, 0)))
    second = second.reshape(8, depth, wrows).transpose(1, 0, 2)
    second = lax.all_to_all(second, "fsdp", 0, 0, tiled=True)
    second, down_grad, proj_term = stage(second, down_grad, proj_term)
    proj_grad = lax.psum_scatter(proj_term, "fsdp", scatter_dimension=0, tiled=True)
    proj_grad, down_grad = proj_grad.astype(F32), down_grad.astype(F32)
    second = jnp.sum(second, 0)
    wide_grads = [second[i] for i in (5, 6, 0, 1, 2, 3)]
    vbias_grad = second[4, : value_bias.shape[0]]
    qbias_grad = second[7]
    return (
        layer_out[None],
        input_grad[None],
        wide_grads[0],
        wide_grads[1],
        qkv_grad,
        qbias_grad,
        vbias_grad,
        proj_grad,
        wide_grads[2],
        wide_grads[3],
        wide_grads[4],
        up_grad,
        ubias_grad,
        down_grad,
        wide_grads[5],
    )


def solution(mesh):
    rows = P("fsdp", "ctx", None)
    vector = P(BOTH)
    matrix = P(BOTH, None)
    return jax.shard_map(
        body,
        mesh=mesh,
        in_specs=(
            rows, rows, P("fsdp"), vector, vector, matrix, vector, vector, matrix,
            vector, vector, vector, matrix, vector, matrix, vector,
        ),
        out_specs=(
            rows, rows, vector, vector, matrix, vector, vector, matrix, vector,
            vector, vector, matrix, vector, matrix, vector,
        ),
        check_vma=False,
    )
```

```python
import functools
import math

import jax
import jax.numpy as jnp
from jax import lax
from jax.experimental import pallas as pl
from jax.experimental.pallas import tpu as pltpu
from jax.sharding import PartitionSpec as P

HEADS = 16
HD = 128
EPS = 1e-05
NEG = -1e30
TILE = 512
BOTH = ("ctx", "fsdp")
BF = jnp.bfloat16
F32 = jnp.float32


def dot(a, b, da, db):
    return lax.dot_general(
        a, b, (((da,), (db,)), ((), ())), preferred_element_type=F32
    )


def normalize(values):
    center = values - jnp.mean(values, -1, keepdims=True)
    inverse = lax.rsqrt(jnp.mean(center * center, -1, keepdims=True) + EPS)
    return center * inverse, inverse


def norm_backward(grad, scaled, inverse, gain):
    inner = grad * gain
    return inverse * (
        inner
        - jnp.mean(inner, -1, keepdims=True)
        - scaled * jnp.mean(inner * scaled, -1, keepdims=True)
    )


def gelu(values):
    return jax.nn.gelu(values, approximate=True)


def attend_kernel(q_ref, k_ref, v_ref, row_limit_ref, key_pos_ref, out_ref):
    scale = 1.0 / math.sqrt(HD)
    allowed = key_pos_ref[...] <= row_limit_ref[...]
    scores = jnp.where(allowed, dot(q_ref[...], k_ref[...], 1, 1) * scale, NEG)
    top = jnp.max(scores, -1, keepdims=True)
    expo = jnp.exp(scores - top)
    probs = expo * (1.0 / jnp.sum(expo, -1, keepdims=True))
    out_ref[...] = dot(probs.astype(BF), v_ref[...], 1, 0).astype(BF)


def attend(queries, keys, values, limit, pos):
    rows = min(TILE, queries.shape[0])
    count = queries.shape[1] // HD - 1
    tile = pl.BlockSpec((rows, HD), lambda h, i: (i, h))
    whole = pl.BlockSpec(keys.shape, lambda h, i: (0, 0))
    return pl.pallas_call(
        attend_kernel,
        grid=(count, queries.shape[0] // rows),
        in_specs=[
            tile,
            whole,
            whole,
            pl.BlockSpec((rows, 1), lambda h, i: (i, 0)),
            pl.BlockSpec((1, keys.shape[0]), lambda h, i: (0, 0)),
        ],
        out_specs=tile,
        out_shape=jax.ShapeDtypeStruct((queries.shape[0], count * HD), BF),
        cost_estimate=pl.CostEstimate(flops=0, bytes_accessed=0, transcendentals=0),
        name="attend",
    )(queries, keys, values, limit[:, None], pos[None, :])


def attend_back_kernel(
    q_ref, k_ref, v_ref, grad_ref, row_limit_ref, key_pos_ref, gq_ref, gk_ref, gv_ref
):
    scale = 1.0 / math.sqrt(HD)

    @pl.when((pl.program_id(0) == 0) & (pl.program_id(1) == 0))
    def _():
        gk_ref[...] = jnp.zeros_like(gk_ref)
        gv_ref[...] = jnp.zeros_like(gv_ref)

    q, k, v, grad = q_ref[...], k_ref[...], v_ref[...], grad_ref[...]
    allowed = key_pos_ref[...] <= row_limit_ref[...]
    scores = jnp.where(allowed, dot(k, q, 1, 1) * scale, NEG)
    top = jnp.max(scores, 0, keepdims=True)
    expo = jnp.exp(scores - top)
    probs = expo * (1.0 / jnp.sum(expo, 0, keepdims=True))
    gv_ref[...] += dot(probs.astype(BF), grad, 1, 0)
    grad_probs = dot(v, grad, 1, 1)
    delta = jnp.sum(probs * grad_probs, 0, keepdims=True)
    grad_scores = (probs * (grad_probs - delta)).astype(BF)
    gk_ref[...] += dot(grad_scores, q, 1, 0) * scale
    gq_ref[...] = (dot(grad_scores, k, 0, 0) * scale).astype(BF)


def attend_back(queries, keys, values, grads, limit, pos):
    rows = min(TILE, queries.shape[0])
    count = queries.shape[1] // HD - 1
    tile = pl.BlockSpec((rows, HD), lambda h, i: (i, h))
    whole = pl.BlockSpec(keys.shape, lambda h, i: (0, 0))
    return pl.pallas_call(
        attend_back_kernel,
        grid=(count, queries.shape[0] // rows),
        in_specs=[
            tile,
            whole,
            whole,
            tile,
            pl.BlockSpec((1, rows), lambda h, i: (0, i)),
            pl.BlockSpec((keys.shape[0], 1), lambda h, i: (0, 0)),
        ],
        out_specs=[tile, whole, whole],
        out_shape=[
            jax.ShapeDtypeStruct((queries.shape[0], count * HD), BF),
            jax.ShapeDtypeStruct(keys.shape, F32),
            jax.ShapeDtypeStruct(keys.shape, F32),
        ],
        cost_estimate=pl.CostEstimate(flops=0, bytes_accessed=0, transcendentals=0),
        name="attend_back",
    )(queries, keys, values, grads, limit[None, :], pos[:, None])


def stage(*values):
    return lax.optimization_barrier(values)


def call(kernel, grid, in_specs, out_specs, out_shape, name):
    return pl.pallas_call(
        kernel,
        grid=grid,
        in_specs=in_specs,
        out_specs=out_specs,
        out_shape=out_shape,
        cost_estimate=pl.CostEstimate(flops=0, bytes_accessed=0, transcendentals=0),
        name=name,
    )


def multiply_kernel(dim, a_ref, b_ref, out_ref):
    out_ref[...] = dot(a_ref[...], b_ref[...], 1, dim).astype(out_ref.dtype)


def multiply(a, b, dim, dtype=F32):
    rows, depth = a.shape
    columns = b.shape[1 - dim]
    tile = min(512, columns)
    if dim:
        b_spec = pl.BlockSpec((tile, depth), lambda j: (j, 0))
    else:
        b_spec = pl.BlockSpec((depth, tile), lambda j: (0, j))
    return call(
        functools.partial(multiply_kernel, dim),
        (columns // tile,),
        [pl.BlockSpec((rows, depth), lambda j: (0, 0)), b_spec],
        pl.BlockSpec((rows, tile), lambda j: (0, j)),
        jax.ShapeDtypeStruct((rows, columns), dtype),
        "multiply",
    )(a, b)


def over_rows_kernel(a0_ref, a1_ref, b0_ref, b1_ref, out_ref):
    total = dot(a0_ref[...], b0_ref[...], 0, 0) + dot(a1_ref[...], b1_ref[...], 0, 0)
    out_ref[...] = total.astype(BF)


def dot_over_rows(lefts, rights):
    rows, height = lefts[0].shape
    width = rights[0].shape[1]
    tile = min(256, height)
    left = pl.BlockSpec((rows, tile), lambda i: (0, i))
    right = pl.BlockSpec((rows, width), lambda i: (0, 0))
    return call(
        over_rows_kernel,
        (height // tile,),
        [left, left, right, right],
        pl.BlockSpec((tile, width), lambda i: (i, 0)),
        jax.ShapeDtypeStruct((height, width), BF),
        "over_rows",
    )(*lefts, *rights)


def plain_over_rows(lefts, rights):
    return (dot(lefts[0], rights[0], 0, 0) + dot(lefts[1], rights[1], 0, 0)).astype(BF)


def hidden_kernel(x0_ref, x1_ref, w_ref, bias_ref, g0_ref, g1_ref, a0_ref, a1_ref, o0_ref, o1_ref):
    root, cubic = math.sqrt(2.0 / math.pi), 0.044715
    halves = (x0_ref, g0_ref, a0_ref, o0_ref), (x1_ref, g1_ref, a1_ref, o1_ref)
    for x_ref, grad_ref, active_ref, out_ref in halves:
        u = dot(x_ref[...], w_ref[...], 1, 0) + bias_ref[...]
        square = u * u
        t = jnp.tanh(root * u * (1.0 + cubic * square))
        active_ref[...] = (0.5 * u * (1.0 + t)).astype(BF)
        slope = 0.5 * (1.0 + t) + 0.5 * u * (1.0 - t * t) * (root * (1.0 + 3.0 * cubic * square))
        out_ref[...] = (grad_ref[...] * slope).astype(BF)


def hidden_layer(halves, weight, bias, grads):
    count, width = halves[0].shape
    columns = weight.shape[1]
    tile = min(256, columns)
    whole = pl.BlockSpec((count, width), lambda j: (0, 0))
    piece = pl.BlockSpec((count, tile), lambda j: (0, j))
    a0, a1, o0, o1 = call(
        hidden_kernel,
        (columns // tile,),
        [
            whole,
            whole,
            pl.BlockSpec((width, tile), lambda j: (0, j)),
            pl.BlockSpec((1, tile), lambda j: (0, j)),
            piece,
            piece,
        ],
        [piece] * 4,
        [jax.ShapeDtypeStruct((count, columns), BF)] * 4,
        "hidden_layer",
    )(*halves, weight, bias[None], *grads)
    return (a0, a1), (o0, o1)


def exchange(value, mask):
    count = lax.axis_size("ctx")
    return lax.ppermute(value, "ctx", [(i, i ^ mask) for i in range(count)])


def chip_groups():
    count = lax.axis_size("ctx")
    return [list(range(core, count, 2)) for core in range(2)]


def chip_devices():
    width = 2 * lax.axis_size("fsdp")
    total = lax.axis_size("ctx") * lax.axis_size("fsdp")
    return [list(range(at, at + width)) for at in range(0, total, width)]


def plane_direct(value):
    chips = lax.axis_size("ctx") // 2
    return [value] + [exchange(value, 2 * k) for k in range(1, chips)]


def both_cores(own):
    return own, exchange(own, 1)


def core_sum(lefts, weight, dim):
    other, early = stage(dot(lefts[1], weight, 1, dim).astype(BF), lefts[0])
    return stage(dot(early, weight, 1, dim), exchange(other, 1))


def plane_parts(halves):
    own, other = halves
    chips = lax.axis_size("ctx") // 2
    rows = own.shape[0] // chips
    parts = [
        own[k * rows : (k + 1) * rows] + other[k * rows : (k + 1) * rows].astype(F32)
        for k in range(chips)
    ]
    return [parts[0]] + [piece.astype(BF) for piece in parts[1:]]


def plane_sum(parts, fill=None):
    chips = lax.axis_size("ctx") // 2
    arrived = [exchange(parts[k], 2 * k) for k in range(1, chips - 1)]
    filled = fill(*parts) if fill else ()
    last = stage(parts[chips - 1], filled)[0]
    total = parts[0]
    for piece in arrived + [exchange(last, 2 * chips - 2)]:
        total = total + piece.astype(F32)
    return total, filled


def turned(value, by):
    depth = lax.axis_size("fsdp")
    return lax.ppermute(value, "fsdp", [(i, (i + by) % depth) for i in range(depth)])


def slot(s):
    depth = lax.axis_size("fsdp")
    return (lax.axis_index("fsdp") - s) % depth


def near_rows(value):
    depth = lax.axis_size("fsdp")
    return {s: turned(value, s) for s in range(1, depth) if s != depth // 2}


def far_rows(value, near):
    depth = lax.axis_size("fsdp")
    pieces = {0: value, **near, depth // 2: turned(value, depth // 2)}
    rows = jnp.zeros((depth,) + value.shape, value.dtype)
    for s, piece in pieces.items():
        rows = lax.dynamic_update_slice(rows, piece[None], (slot(s), 0, 0))
    return rows.reshape(depth * value.shape[0], value.shape[1])


def column_parts(own, other=None):
    depth = lax.axis_size("fsdp")
    rows = own.shape[0] // depth
    parts = []
    for s in range(depth):
        part = lax.dynamic_slice_in_dim(own, slot(s) * rows, rows, 0)
        if other is not None:
            theirs = lax.dynamic_slice_in_dim(other, slot(s) * rows, rows, 0)
            part = part + theirs.astype(F32)
        parts.append(part.astype(BF) if s else part.astype(F32))
    return parts


def column_near(parts):
    depth = len(parts)
    return [parts[0]] + [turned(parts[s], -s) for s in range(1, depth) if s != depth // 2]


def column_far(parts, near):
    middle = len(parts) // 2
    total = turned(parts[middle], -middle).astype(F32)
    for piece in near:
        total = total + piece.astype(F32)
    return total


def lay_out(vectors, width):
    row, column, laid, places = 0, 0, 0, []
    for v in vectors:
        n = v.shape[0]
        if column + n > width:
            row, column = row + 1, 0
        places.append((row, column, n))
        laid = laid + jnp.pad(v[None], ((row, 7 - row), (column, width - column - n)))
        column += -(-n // 128) * 128
    return laid, places


def body(
    hidden_in,
    out_cotangent,
    seq_lengths,
    first_gain,
    first_shift,
    qkv_weight,
    query_bias,
    value_bias,
    proj_weight,
    proj_bias,
    second_gain,
    second_shift,
    up_weight,
    up_bias,
    down_weight,
    down_bias,
):
    count, depth = lax.axis_size("ctx"), lax.axis_size("fsdp")
    chips = count // 2
    at, level = lax.axis_index("ctx"), lax.axis_index("fsdp")
    core, chip = at % 2, at // 2
    span, width = hidden_in.shape[1:]
    wrows = qkv_weight.shape[0]
    hidden = up_weight.shape[1]
    frows = down_weight.shape[0]
    share = HEADS // count
    qcols = share * HD
    wide_cols = qcols + HD
    total = span * count
    length = seq_lengths[0]
    positions = at * span + jnp.arange(span, dtype=jnp.int32)
    live = (positions < length)[:, None]

    small = [
        first_gain,
        first_shift,
        query_bias,
        value_bias,
        proj_bias,
        second_gain,
        second_shift,
        up_bias,
        down_bias,
    ]
    packed, places = lay_out(small, wide_cols)
    qpart = qkv_weight[:, :width].reshape(wrows, count, qcols).transpose(1, 0, 2)
    kvpart = qkv_weight[:, width:].reshape(wrows, 2, HD).transpose(1, 0, 2)
    kvpart = jnp.broadcast_to(kvpart[None], (chips, 2, wrows, HD)).reshape(count, wrows, HD)
    outgoing = jnp.concatenate(
        [
            jnp.concatenate([qpart, kvpart], 2),
            jnp.broadcast_to(packed[None], (count,) + packed.shape),
        ],
        1,
    )
    incoming = lax.all_to_all(outgoing, "ctx", 0, 0, tiled=True)
    incoming, hidden_own, upstream = stage(incoming, hidden_in[0], out_cotangent[0])

    attn_all = lax.all_gather(incoming, "fsdp", axis=0)
    row_pieces = plane_direct(hidden_own)
    row_halves = both_cores(jnp.concatenate(row_pieces, 0))
    down_pieces = plane_direct(stage(down_weight, row_pieces)[0])
    own_rows = hidden_own.astype(F32)
    upstream = jnp.where(live, upstream.astype(F32), 0.0)
    grad_mlp_own = upstream.astype(BF)
    attn_all, row_halves, grad_mlp_own, proj_own, up_own = stage(
        attn_all, row_halves, grad_mlp_own, proj_weight, up_weight
    )

    proj_local = lax.all_gather(proj_own, "fsdp", axis=0, tiled=True)
    mlp_rows = lax.all_gather(grad_mlp_own, "fsdp", axis=0, tiled=True)
    up_parts = (
        up_own.reshape(wrows, chips, 2 * depth, frows)
        .transpose(2, 0, 1, 3)
        .reshape(2 * depth, wrows, chips * frows)
    )
    up_parts = lax.all_to_all(
        up_parts, BOTH, 0, 0, tiled=True, axis_index_groups=chip_devices()
    ).reshape(2 * depth * wrows, chips * frows)
    attn_rows = attn_all.transpose(1, 0, 2, 3)
    qkv_local = attn_rows[:, :, :wrows].reshape(width, wide_cols)
    table = attn_rows[:, :, wrows:].reshape(count * depth, 8, wide_cols)
    vectors = [table[:, r, c : c + n].reshape(-1).astype(F32) for r, c, n in places]
    gain_one, shift_one, qbias, vbias, pbias, gain_two, shift_two, ubias, dbias = vectors
    ubias = lax.dynamic_slice(
        ubias.reshape(chips, 2 * depth, frows), (0, core * depth + level, 0), (chips, 1, frows)
    ).reshape(-1)
    bias_one = jnp.concatenate(
        [
            lax.dynamic_slice(qbias, (at * qcols,), (qcols,)),
            jnp.where(core == 1, vbias, 0.0),
        ]
    )
    normed_one = [
        (normalize(half.astype(F32))[0] * gain_one + shift_one).astype(BF) for half in row_halves
    ]
    mixed = jnp.concatenate([dot(half, qkv_local, 1, 0) for half in normed_one], 0)
    queries = (mixed + bias_one).astype(BF)
    mine = queries[:, qcols:]
    theirs = jnp.roll(exchange(mine, 1), total // 2, 0)
    keys = jnp.where(core == 0, mine, theirs)
    values = jnp.where(core == 0, theirs, mine)
    base = jnp.stack([at ^ (2 * k + j) for j in range(2) for k in range(chips)]) * span
    pos = (base[:, None] + jnp.arange(span, dtype=jnp.int32)[None]).reshape(total)
    limit = jnp.minimum(pos, length - 1)
    attended = attend(queries, keys, values, limit, pos)
    held = (pbias, gain_two, shift_two, ubias, dbias)
    attended, up_parts, held, proj_local, down_pieces = stage(
        attended, up_parts, held, proj_local, down_pieces
    )
    pbias, gain_two, shift_two, ubias, dbias = held

    attended_halves = attended[: total // 2], attended[total // 2 :]
    down_local = jnp.zeros((chips, frows, width), BF)
    for k, piece in enumerate(down_pieces):
        down_local = lax.dynamic_update_slice(down_local, piece[None], (chip ^ k, 0, 0))
    down_local = down_local.reshape(chips * frows, width)
    branch, _ = plane_sum(plane_parts(core_sum(attended_halves, proj_local, 0)))
    middle = own_rows + branch + pbias
    scaled_two, inverse_two = normalize(middle)
    normed_two_own = (scaled_two * gain_two + shift_two).astype(BF)
    normed_two_own, down_local, up_parts, mlp_rows = stage(
        normed_two_own, down_local, up_parts, mlp_rows
    )

    up_local = lax.all_gather(
        up_parts, "ctx", axis=0, tiled=True, axis_index_groups=chip_groups()
    )

    near = near_rows(normed_two_own)
    mlp_halves = both_cores(mlp_rows)
    grad_active = [multiply(half, down_local, 1) for half in mlp_halves]
    near, normed_value, mlp_halves, grad_active = stage(
        near, normed_two_own, mlp_halves, grad_active
    )
    normed_rows = far_rows(normed_value, near)
    normed_rows = stage(normed_rows)[0]

    normed_halves = both_cores(normed_rows)
    active, grad_before = hidden_layer(normed_halves, up_local, ubias, grad_active)

    def chip_sum(term):
        return lax.psum_scatter(
            term, "ctx", scatter_dimension=0, tiled=True, axis_index_groups=chip_groups()
        )

    two_parts = column_parts(*core_sum(grad_before, up_local, 1))

    held = stage(normed_halves, grad_before, active, mlp_halves, two_parts)
    normed, grads, acts, mlps = held[:4]
    out_other = multiply(acts[1], down_local, 0, BF)
    out_own = multiply(acts[0], down_local, 0)
    up_term = dot_over_rows(normed, grads)
    near, two_parts, up_term, out_own, out_other = stage(
        column_near(two_parts), two_parts, up_term, out_own, out_other
    )
    out_term = (out_own + exchange(out_other, 1).astype(F32)).astype(BF)
    up_grad = chip_sum(up_term)
    acts, mlps, grads = stage(acts, mlps, grads, near)[:3]
    down_term = dot_over_rows(acts, mlps)
    ubias_term = jnp.sum(grads[0].astype(F32), 0) + jnp.sum(grads[1].astype(F32), 0)
    grad_two = column_far(two_parts, near)
    gain_two_term = jnp.sum(grad_two * scaled_two, 0)
    shift_two_term = jnp.sum(grad_two, 0)
    grad_middle = upstream + norm_backward(grad_two, scaled_two, inverse_two, gain_two)
    grad_branch_own = grad_middle.astype(BF)
    grad_branch_own, out_term, down_term, ubias_term = stage(
        grad_branch_own, out_term, down_term, ubias_term
    )
    out_sum = lax.psum_scatter(out_term, "fsdp", scatter_dimension=0, tiled=True)

    branch_halves = both_cores(jnp.concatenate(plane_direct(grad_branch_own), 0))
    pbias_term = jnp.sum(grad_branch_own.astype(F32), 0)
    dbias_term = jnp.sum(grad_mlp_own.astype(F32), 0)
    branch_halves, pbias_term, dbias_term, up_grad = stage(
        branch_halves, pbias_term, dbias_term, up_grad
    )

    grad_attended = jnp.concatenate(
        [dot(half, proj_local, 1, 1) for half in branch_halves], 0
    ).astype(BF)
    grad_queries, grad_keys, grad_values = attend_back(
        queries, keys, values, grad_attended, limit, pos
    )
    given = jnp.where(core == 0, grad_values, grad_keys).astype(BF)
    given = jnp.roll(exchange(given, 1), total // 2, 0).astype(F32)
    grad_kind = (jnp.where(core == 0, grad_keys, grad_values) + given).astype(BF)
    grad_mixed = jnp.concatenate([grad_queries, grad_kind], 1)

    grad_mixed, down_term = stage(grad_mixed, down_term)
    down_grad = chip_sum(down_term)

    mixed_halves = grad_mixed[: total // 2], grad_mixed[total // 2 :]
    proj_term = plain_over_rows(attended_halves, branch_halves)
    one_sums = core_sum(mixed_halves, qkv_local, 1)
    one_sums, proj_term, out_sum = stage(one_sums, proj_term, out_sum)
    one_parts = plane_parts(one_sums)
    up_grad = stage(up_grad, one_parts)[0]
    up_grad = lax.all_to_all(
        up_grad.reshape(2 * depth, wrows, chips * frows),
        BOTH,
        0,
        0,
        tiled=True,
        axis_index_groups=chip_devices(),
    )

    def qkv_parts(*gate):
        halves = stage(mixed_halves, gate)[0]
        term = plain_over_rows(normed_one, halves)
        term = term.reshape(count, depth, wrows, wide_cols).transpose(1, 0, 2, 3)
        return column_parts(term.reshape(depth * count * wrows, wide_cols))

    grad_one, qkv_term = plane_sum(one_parts, qkv_parts)
    qkv_near = column_near(qkv_term)
    scaled_one, inverse_one = normalize(own_rows)
    gain_one_term = jnp.sum(grad_one * scaled_one, 0)
    shift_one_term = jnp.sum(grad_one, 0)
    held = (grad_one, qkv_term, qkv_near, up_grad, proj_term)
    gain_one_term, shift_one_term, held = stage(gain_one_term, shift_one_term, held)
    grad_one, qkv_term, qkv_near, up_grad, proj_term = held

    result = middle + out_sum.astype(F32) + dbias
    layer_out = jnp.where(live, result, 0.0).astype(BF)
    qkv_grad = column_far(qkv_term, qkv_near).astype(BF)
    qkv_grad = qkv_grad.reshape(count, wrows, wide_cols)
    input_grad = grad_middle + norm_backward(grad_one, scaled_one, inverse_one, gain_one)
    up_grad = (
        up_grad.reshape(2 * depth, wrows, chips, frows)
        .transpose(1, 2, 0, 3)
        .reshape(wrows, hidden)
        .astype(F32)
    )
    qkv_grad = lax.all_to_all(qkv_grad, "ctx", 0, 0, tiled=True).transpose(1, 0, 2).astype(F32)
    kinds = jnp.sum(qkv_grad[:, :, qcols:].reshape(wrows, chips, 2 * HD), 1)
    qkv_grad = jnp.concatenate([qkv_grad[:, :, :qcols].reshape(wrows, width), kinds], 1)

    mixed_term = jnp.sum(grad_mixed.astype(F32), 0)
    vbias_term = jnp.where(core == 1, mixed_term[qcols:], 0.0).reshape(count * depth, -1)
    vbias_term = jnp.pad(vbias_term, ((0, 0), (0, wrows - vbias_term.shape[1]))).reshape(-1)
    ubias_term = ubias_term.reshape(chips, 1, frows)
    ubias_term = jnp.where(jnp.arange(2)[None, :, None] == core, ubias_term, 0.0)
    terms = [pbias_term, gain_two_term, shift_two_term, dbias_term, vbias_term]
    early = jnp.stack(terms + [jnp.zeros_like(vbias_term)] * 3)
    early = early.reshape(8, count, -1)
    ub = jnp.pad(ubias_term.reshape(1, count, frows), ((0, 7), (0, 0), (0, 0)))
    early, ub = early.transpose(1, 0, 2), ub.transpose(1, 0, 2)
    late = jnp.stack([gain_one_term, shift_one_term]).reshape(2, count, -1).transpose(1, 0, 2)
    late = jnp.pad(late, ((0, 0), (5, 1), (0, 0)))
    block = late.shape[2]
    first = lax.all_to_all(
        jnp.concatenate([early + late, ub], 2), "ctx", 0, 0, tiled=True
    )
    down_grad, proj_term = stage(down_grad, proj_term, first)[:2]
    proj_grad = lax.psum_scatter(proj_term, "fsdp", scatter_dimension=0, tiled=True)
    proj_grad, down_grad = proj_grad.astype(F32), down_grad.astype(F32)
    first = jnp.sum(first, 0)
    ubias_grad = first[0, block:]
    second = first[:, :block] + jnp.pad(mixed_term[None, :qcols], ((7, 0), (0, 0)))
    second = second.reshape(8, depth, wrows).transpose(1, 0, 2)
    second = lax.all_to_all(second, "fsdp", 0, 0, tiled=True)
    second = jnp.sum(second, 0)
    wide_grads = [second[i] for i in (5, 6, 0, 1, 2, 3)]
    vbias_grad = second[4, : value_bias.shape[0]]
    qbias_grad = second[7]
    return (
        layer_out[None],
        input_grad[None],
        wide_grads[0],
        wide_grads[1],
        qkv_grad,
        qbias_grad,
        vbias_grad,
        proj_grad,
        wide_grads[2],
        wide_grads[3],
        wide_grads[4],
        up_grad,
        ubias_grad,
        down_grad,
        wide_grads[5],
    )


def solution(mesh):
    rows = P("fsdp", "ctx", None)
    vector = P(BOTH)
    matrix = P(BOTH, None)
    return jax.shard_map(
        body,
        mesh=mesh,
        in_specs=(
            rows, rows, P("fsdp"), vector, vector, matrix, vector, vector, matrix,
            vector, vector, vector, matrix, vector, matrix, vector,
        ),
        out_specs=(
            rows, rows, vector, vector, matrix, vector, vector, matrix, vector,
            vector, vector, matrix, vector, matrix, vector,
        ),
        check_vma=False,
    )
```

```python
import functools
import math

import jax
import jax.numpy as jnp
from jax import lax
from jax.experimental import pallas as pl
from jax.experimental.pallas import tpu as pltpu
from jax.sharding import PartitionSpec as P

HEADS = 16
HD = 128
EPS = 1e-05
NEG = -1e30
TILE = 512
BOTH = ("ctx", "fsdp")
BF = jnp.bfloat16
F32 = jnp.float32


def dot(a, b, da, db):
    return lax.dot_general(
        a, b, (((da,), (db,)), ((), ())), preferred_element_type=F32
    )


def normalize(values):
    center = values - jnp.mean(values, -1, keepdims=True)
    inverse = lax.rsqrt(jnp.mean(center * center, -1, keepdims=True) + EPS)
    return center * inverse, inverse


def norm_backward(grad, scaled, inverse, gain):
    inner = grad * gain
    return inverse * (
        inner
        - jnp.mean(inner, -1, keepdims=True)
        - scaled * jnp.mean(inner * scaled, -1, keepdims=True)
    )


def gelu(values):
    return jax.nn.gelu(values, approximate=True)


def attend_kernel(q_ref, k_ref, v_ref, row_limit_ref, key_pos_ref, out_ref):
    scale = 1.0 / math.sqrt(HD)
    allowed = key_pos_ref[...] <= row_limit_ref[...]
    scores = jnp.where(allowed, dot(q_ref[...], k_ref[...], 1, 1) * scale, NEG)
    top = jnp.max(scores, -1, keepdims=True)
    expo = jnp.exp(scores - top)
    probs = expo * (1.0 / jnp.sum(expo, -1, keepdims=True))
    out_ref[...] = dot(probs.astype(BF), v_ref[...], 1, 0).astype(BF)


def attend(queries, keys, values, limit, pos):
    rows = min(TILE, queries.shape[0])
    count = queries.shape[1] // HD - 1
    tile = pl.BlockSpec((rows, HD), lambda h, i: (i, h))
    whole = pl.BlockSpec(keys.shape, lambda h, i: (0, 0))
    return pl.pallas_call(
        attend_kernel,
        grid=(count, queries.shape[0] // rows),
        in_specs=[
            tile,
            whole,
            whole,
            pl.BlockSpec((rows, 1), lambda h, i: (i, 0)),
            pl.BlockSpec((1, keys.shape[0]), lambda h, i: (0, 0)),
        ],
        out_specs=tile,
        out_shape=jax.ShapeDtypeStruct((queries.shape[0], count * HD), BF),
        cost_estimate=pl.CostEstimate(flops=0, bytes_accessed=0, transcendentals=0),
        name="attend",
    )(queries, keys, values, limit[:, None], pos[None, :])


def attend_back_kernel(
    q_ref, k_ref, v_ref, grad_ref, row_limit_ref, key_pos_ref, gq_ref, gk_ref, gv_ref
):
    scale = 1.0 / math.sqrt(HD)

    @pl.when((pl.program_id(0) == 0) & (pl.program_id(1) == 0))
    def _():
        gk_ref[...] = jnp.zeros_like(gk_ref)
        gv_ref[...] = jnp.zeros_like(gv_ref)

    q, k, v, grad = q_ref[...], k_ref[...], v_ref[...], grad_ref[...]
    allowed = key_pos_ref[...] <= row_limit_ref[...]
    scores = jnp.where(allowed, dot(k, q, 1, 1) * scale, NEG)
    top = jnp.max(scores, 0, keepdims=True)
    expo = jnp.exp(scores - top)
    probs = expo * (1.0 / jnp.sum(expo, 0, keepdims=True))
    gv_ref[...] += dot(probs.astype(BF), grad, 1, 0)
    grad_probs = dot(v, grad, 1, 1)
    delta = jnp.sum(probs * grad_probs, 0, keepdims=True)
    grad_scores = (probs * (grad_probs - delta)).astype(BF)
    gk_ref[...] += dot(grad_scores, q, 1, 0) * scale
    gq_ref[...] = (dot(grad_scores, k, 0, 0) * scale).astype(BF)


def attend_back(queries, keys, values, grads, limit, pos):
    rows = min(TILE, queries.shape[0])
    count = queries.shape[1] // HD - 1
    tile = pl.BlockSpec((rows, HD), lambda h, i: (i, h))
    whole = pl.BlockSpec(keys.shape, lambda h, i: (0, 0))
    return pl.pallas_call(
        attend_back_kernel,
        grid=(count, queries.shape[0] // rows),
        in_specs=[
            tile,
            whole,
            whole,
            tile,
            pl.BlockSpec((1, rows), lambda h, i: (0, i)),
            pl.BlockSpec((keys.shape[0], 1), lambda h, i: (0, 0)),
        ],
        out_specs=[tile, whole, whole],
        out_shape=[
            jax.ShapeDtypeStruct((queries.shape[0], count * HD), BF),
            jax.ShapeDtypeStruct(keys.shape, F32),
            jax.ShapeDtypeStruct(keys.shape, F32),
        ],
        cost_estimate=pl.CostEstimate(flops=0, bytes_accessed=0, transcendentals=0),
        name="attend_back",
    )(queries, keys, values, grads, limit[None, :], pos[:, None])


def stage(*values):
    return lax.optimization_barrier(values)


def call(kernel, grid, in_specs, out_specs, out_shape, name):
    return pl.pallas_call(
        kernel,
        grid=grid,
        in_specs=in_specs,
        out_specs=out_specs,
        out_shape=out_shape,
        cost_estimate=pl.CostEstimate(flops=0, bytes_accessed=0, transcendentals=0),
        name=name,
    )


def multiply_kernel(dim, a_ref, b_ref, out_ref):
    out_ref[...] = dot(a_ref[...], b_ref[...], 1, dim).astype(out_ref.dtype)


def multiply(a, b, dim, dtype=F32):
    rows, depth = a.shape
    columns = b.shape[1 - dim]
    tile = min(512, columns)
    if dim:
        b_spec = pl.BlockSpec((tile, depth), lambda j: (j, 0))
    else:
        b_spec = pl.BlockSpec((depth, tile), lambda j: (0, j))
    return call(
        functools.partial(multiply_kernel, dim),
        (columns // tile,),
        [pl.BlockSpec((rows, depth), lambda j: (0, 0)), b_spec],
        pl.BlockSpec((rows, tile), lambda j: (0, j)),
        jax.ShapeDtypeStruct((rows, columns), dtype),
        "multiply",
    )(a, b)


def over_rows_kernel(a0_ref, a1_ref, b0_ref, b1_ref, out_ref):
    total = dot(a0_ref[...], b0_ref[...], 0, 0) + dot(a1_ref[...], b1_ref[...], 0, 0)
    out_ref[...] = total.astype(BF)


def dot_over_rows(lefts, rights):
    rows, height = lefts[0].shape
    width = rights[0].shape[1]
    tile = min(256, height)
    left = pl.BlockSpec((rows, tile), lambda i: (0, i))
    right = pl.BlockSpec((rows, width), lambda i: (0, 0))
    return call(
        over_rows_kernel,
        (height // tile,),
        [left, left, right, right],
        pl.BlockSpec((tile, width), lambda i: (i, 0)),
        jax.ShapeDtypeStruct((height, width), BF),
        "over_rows",
    )(*lefts, *rights)


def plain_over_rows(lefts, rights):
    return (dot(lefts[0], rights[0], 0, 0) + dot(lefts[1], rights[1], 0, 0)).astype(BF)


def hidden_kernel(x0_ref, x1_ref, w_ref, bias_ref, g0_ref, g1_ref, a0_ref, a1_ref, o0_ref, o1_ref):
    root, cubic = math.sqrt(2.0 / math.pi), 0.044715
    halves = (x0_ref, g0_ref, a0_ref, o0_ref), (x1_ref, g1_ref, a1_ref, o1_ref)
    for x_ref, grad_ref, active_ref, out_ref in halves:
        u = dot(x_ref[...], w_ref[...], 1, 0) + bias_ref[...]
        square = u * u
        t = jnp.tanh(root * u * (1.0 + cubic * square))
        active_ref[...] = (0.5 * u * (1.0 + t)).astype(BF)
        slope = 0.5 * (1.0 + t) + 0.5 * u * (1.0 - t * t) * (root * (1.0 + 3.0 * cubic * square))
        out_ref[...] = (grad_ref[...] * slope).astype(BF)


def hidden_layer(halves, weight, bias, grads):
    count, width = halves[0].shape
    columns = weight.shape[1]
    tile = min(256, columns)
    whole = pl.BlockSpec((count, width), lambda j: (0, 0))
    piece = pl.BlockSpec((count, tile), lambda j: (0, j))
    a0, a1, o0, o1 = call(
        hidden_kernel,
        (columns // tile,),
        [
            whole,
            whole,
            pl.BlockSpec((width, tile), lambda j: (0, j)),
            pl.BlockSpec((1, tile), lambda j: (0, j)),
            piece,
            piece,
        ],
        [piece] * 4,
        [jax.ShapeDtypeStruct((count, columns), BF)] * 4,
        "hidden_layer",
    )(*halves, weight, bias[None], *grads)
    return (a0, a1), (o0, o1)


def exchange(value, mask):
    count = lax.axis_size("ctx")
    return lax.ppermute(value, "ctx", [(i, i ^ mask) for i in range(count)])


def chip_groups():
    count = lax.axis_size("ctx")
    return [list(range(core, count, 2)) for core in range(2)]


def chip_devices():
    width = 2 * lax.axis_size("fsdp")
    total = lax.axis_size("ctx") * lax.axis_size("fsdp")
    return [list(range(at, at + width)) for at in range(0, total, width)]


def plane_direct(value):
    chips = lax.axis_size("ctx") // 2
    return [value] + [exchange(value, 2 * k) for k in range(1, chips)]


def both_cores(own):
    return own, exchange(own, 1)


def core_sum(lefts, weight, dim):
    other, early = stage(dot(lefts[1], weight, 1, dim).astype(BF), lefts[0])
    return stage(dot(early, weight, 1, dim), exchange(other, 1))


def plane_parts(halves):
    own, other = halves
    chips = lax.axis_size("ctx") // 2
    rows = own.shape[0] // chips
    parts = [
        own[k * rows : (k + 1) * rows] + other[k * rows : (k + 1) * rows].astype(F32)
        for k in range(chips)
    ]
    return [parts[0]] + [piece.astype(BF) for piece in parts[1:]]


def plane_sum(parts, fill=None):
    chips = lax.axis_size("ctx") // 2
    arrived = [exchange(parts[k], 2 * k) for k in range(1, chips - 1)]
    filled = fill(*parts) if fill else ()
    last = stage(parts[chips - 1], filled)[0]
    total = parts[0]
    for piece in arrived + [exchange(last, 2 * chips - 2)]:
        total = total + piece.astype(F32)
    return total, filled


def turned(value, by):
    depth = lax.axis_size("fsdp")
    return lax.ppermute(value, "fsdp", [(i, (i + by) % depth) for i in range(depth)])


def slot(s):
    depth = lax.axis_size("fsdp")
    return (lax.axis_index("fsdp") - s) % depth


def near_rows(value):
    depth = lax.axis_size("fsdp")
    return {s: turned(value, s) for s in range(1, depth) if s != depth // 2}


def far_rows(value, near):
    depth = lax.axis_size("fsdp")
    pieces = {0: value, **near, depth // 2: turned(value, depth // 2)}
    rows = jnp.zeros((depth,) + value.shape, value.dtype)
    for s, piece in pieces.items():
        rows = lax.dynamic_update_slice(rows, piece[None], (slot(s), 0, 0))
    return rows.reshape(depth * value.shape[0], value.shape[1])


def column_parts(own, other=None):
    depth = lax.axis_size("fsdp")
    rows = own.shape[0] // depth
    parts = []
    for s in range(depth):
        part = lax.dynamic_slice_in_dim(own, slot(s) * rows, rows, 0)
        if other is not None:
            theirs = lax.dynamic_slice_in_dim(other, slot(s) * rows, rows, 0)
            part = part + theirs.astype(F32)
        parts.append(part.astype(BF) if s else part.astype(F32))
    return parts


def column_near(parts):
    depth = len(parts)
    return [parts[0]] + [turned(parts[s], -s) for s in range(1, depth) if s != depth // 2]


def column_far(parts, near):
    middle = len(parts) // 2
    total = turned(parts[middle], -middle).astype(F32)
    for piece in near:
        total = total + piece.astype(F32)
    return total


def lay_out(vectors, width):
    row, column, laid, places = 0, 0, 0, []
    for v in vectors:
        n = v.shape[0]
        if column + n > width:
            row, column = row + 1, 0
        places.append((row, column, n))
        laid = laid + jnp.pad(v[None], ((row, 7 - row), (column, width - column - n)))
        column += -(-n // 128) * 128
    return laid, places


def body(
    hidden_in,
    out_cotangent,
    seq_lengths,
    first_gain,
    first_shift,
    qkv_weight,
    query_bias,
    value_bias,
    proj_weight,
    proj_bias,
    second_gain,
    second_shift,
    up_weight,
    up_bias,
    down_weight,
    down_bias,
):
    count, depth = lax.axis_size("ctx"), lax.axis_size("fsdp")
    chips = count // 2
    at, level = lax.axis_index("ctx"), lax.axis_index("fsdp")
    core, chip = at % 2, at // 2
    span, width = hidden_in.shape[1:]
    wrows = qkv_weight.shape[0]
    hidden = up_weight.shape[1]
    frows = down_weight.shape[0]
    share = HEADS // count
    qcols = share * HD
    wide_cols = qcols + HD
    total = span * count
    length = seq_lengths[0]
    positions = at * span + jnp.arange(span, dtype=jnp.int32)
    live = (positions < length)[:, None]

    small = [
        first_gain,
        first_shift,
        query_bias,
        value_bias,
        proj_bias,
        second_gain,
        second_shift,
        up_bias,
        down_bias,
    ]
    packed, places = lay_out(small, wide_cols)
    qpart = qkv_weight[:, :width].reshape(wrows, count, qcols).transpose(1, 0, 2)
    kvpart = qkv_weight[:, width:].reshape(wrows, 2, HD).transpose(1, 0, 2)
    kvpart = jnp.broadcast_to(kvpart[None], (chips, 2, wrows, HD)).reshape(count, wrows, HD)
    outgoing = jnp.concatenate(
        [
            jnp.concatenate([qpart, kvpart], 2),
            jnp.broadcast_to(packed[None], (count,) + packed.shape),
        ],
        1,
    )
    incoming = lax.all_to_all(outgoing, "ctx", 0, 0, tiled=True)
    incoming, hidden_own, upstream = stage(incoming, hidden_in[0], out_cotangent[0])

    attn_all = lax.all_gather(incoming, "fsdp", axis=0)
    row_pieces = plane_direct(hidden_own)
    row_halves = both_cores(jnp.concatenate(row_pieces, 0))
    down_pieces = plane_direct(stage(down_weight, row_pieces)[0])
    own_rows = hidden_own.astype(F32)
    upstream = jnp.where(live, upstream.astype(F32), 0.0)
    grad_mlp_own = upstream.astype(BF)
    up_parts = (
        up_weight.reshape(wrows, chips, 2 * depth, frows)
        .transpose(2, 0, 1, 3)
        .reshape(2 * depth, wrows, chips * frows)
    )
    attn_all, row_halves, grad_mlp_own, proj_own, up_parts = stage(
        attn_all, row_halves, grad_mlp_own, proj_weight, up_parts
    )

    proj_local = lax.all_gather(proj_own, "fsdp", axis=0, tiled=True)
    mlp_rows = lax.all_gather(grad_mlp_own, "fsdp", axis=0, tiled=True)
    up_parts = lax.all_to_all(
        up_parts, BOTH, 0, 0, tiled=True, axis_index_groups=chip_devices()
    ).reshape(2 * depth * wrows, chips * frows)
    attn_rows = attn_all.transpose(1, 0, 2, 3)
    qkv_local = attn_rows[:, :, :wrows].reshape(width, wide_cols)
    table = attn_rows[:, :, wrows:].reshape(count * depth, 8, wide_cols)
    vectors = [table[:, r, c : c + n].reshape(-1).astype(F32) for r, c, n in places]
    gain_one, shift_one, qbias, vbias, pbias, gain_two, shift_two, ubias, dbias = vectors
    ubias = lax.dynamic_slice(
        ubias.reshape(chips, 2 * depth, frows), (0, core * depth + level, 0), (chips, 1, frows)
    ).reshape(-1)
    bias_one = jnp.concatenate(
        [
            lax.dynamic_slice(qbias, (at * qcols,), (qcols,)),
            jnp.where(core == 1, vbias, 0.0),
        ]
    )
    normed_one = [
        (normalize(half.astype(F32))[0] * gain_one + shift_one).astype(BF) for half in row_halves
    ]
    mixed = jnp.concatenate([dot(half, qkv_local, 1, 0) for half in normed_one], 0)
    queries = (mixed + bias_one).astype(BF)
    mine = queries[:, qcols:]
    theirs = jnp.roll(exchange(mine, 1), total // 2, 0)
    keys = jnp.where(core == 0, mine, theirs)
    values = jnp.where(core == 0, theirs, mine)
    base = jnp.stack([at ^ (2 * k + j) for j in range(2) for k in range(chips)]) * span
    pos = (base[:, None] + jnp.arange(span, dtype=jnp.int32)[None]).reshape(total)
    limit = jnp.minimum(pos, length - 1)
    attended = attend(queries, keys, values, limit, pos)
    held = (pbias, gain_two, shift_two, ubias, dbias)
    attended, up_parts, held, proj_local, down_pieces = stage(
        attended, up_parts, held, proj_local, down_pieces
    )
    pbias, gain_two, shift_two, ubias, dbias = held

    attended_halves = attended[: total // 2], attended[total // 2 :]
    down_local = jnp.zeros((chips, frows, width), BF)
    for k, piece in enumerate(down_pieces):
        down_local = lax.dynamic_update_slice(down_local, piece[None], (chip ^ k, 0, 0))
    down_local = down_local.reshape(chips * frows, width)
    branch, _ = plane_sum(plane_parts(core_sum(attended_halves, proj_local, 0)))
    middle = own_rows + branch + pbias
    scaled_two, inverse_two = normalize(middle)
    normed_two_own = (scaled_two * gain_two + shift_two).astype(BF)
    normed_two_own, down_local, up_parts, mlp_rows = stage(
        normed_two_own, down_local, up_parts, mlp_rows
    )

    up_local = lax.all_gather(
        up_parts, "ctx", axis=0, tiled=True, axis_index_groups=chip_groups()
    )

    near = near_rows(normed_two_own)
    mlp_halves = both_cores(mlp_rows)
    grad_active = [multiply(half, down_local, 1) for half in mlp_halves]
    near, normed_value, mlp_halves, grad_active = stage(
        near, normed_two_own, mlp_halves, grad_active
    )
    normed_rows = far_rows(normed_value, near)
    normed_rows = stage(normed_rows)[0]

    normed_halves = both_cores(normed_rows)
    active, grad_before = hidden_layer(normed_halves, up_local, ubias, grad_active)

    def chip_sum(term):
        return lax.psum_scatter(
            term, "ctx", scatter_dimension=0, tiled=True, axis_index_groups=chip_groups()
        )

    two_parts = column_parts(*core_sum(grad_before, up_local, 1))

    held = stage(normed_halves, grad_before, active, mlp_halves, two_parts)
    normed, grads, acts, mlps = held[:4]
    out_other = multiply(acts[1], down_local, 0, BF)
    out_own = multiply(acts[0], down_local, 0)
    up_term = dot_over_rows(normed, grads)
    near, two_parts, up_term, out_own, out_other = stage(
        column_near(two_parts), two_parts, up_term, out_own, out_other
    )
    out_term = (out_own + exchange(out_other, 1).astype(F32)).astype(BF)
    up_grad = chip_sum(up_term)
    acts, mlps, grads = stage(acts, mlps, grads, near)[:3]
    down_term = dot_over_rows(acts, mlps)
    ubias_term = jnp.sum(grads[0].astype(F32), 0) + jnp.sum(grads[1].astype(F32), 0)
    grad_two = column_far(two_parts, near)
    gain_two_term = jnp.sum(grad_two * scaled_two, 0)
    shift_two_term = jnp.sum(grad_two, 0)
    grad_middle = upstream + norm_backward(grad_two, scaled_two, inverse_two, gain_two)
    grad_branch_own = grad_middle.astype(BF)
    grad_branch_own, out_term, down_term, ubias_term = stage(
        grad_branch_own, out_term, down_term, ubias_term
    )
    out_sum = lax.psum_scatter(out_term, "fsdp", scatter_dimension=0, tiled=True)

    branch_halves = both_cores(jnp.concatenate(plane_direct(grad_branch_own), 0))
    pbias_term = jnp.sum(grad_branch_own.astype(F32), 0)
    dbias_term = jnp.sum(grad_mlp_own.astype(F32), 0)
    branch_halves, pbias_term, dbias_term, up_grad = stage(
        branch_halves, pbias_term, dbias_term, up_grad
    )

    grad_attended = jnp.concatenate(
        [dot(half, proj_local, 1, 1) for half in branch_halves], 0
    ).astype(BF)
    grad_queries, grad_keys, grad_values = attend_back(
        queries, keys, values, grad_attended, limit, pos
    )
    given = jnp.where(core == 0, grad_values, grad_keys).astype(BF)
    given = jnp.roll(exchange(given, 1), total // 2, 0).astype(F32)
    grad_kind = (jnp.where(core == 0, grad_keys, grad_values) + given).astype(BF)
    grad_mixed = jnp.concatenate([grad_queries, grad_kind], 1)

    grad_mixed, down_term = stage(grad_mixed, down_term)
    down_grad = chip_sum(down_term)

    mixed_halves = grad_mixed[: total // 2], grad_mixed[total // 2 :]
    proj_term = plain_over_rows(attended_halves, branch_halves)
    one_sums = core_sum(mixed_halves, qkv_local, 1)
    one_sums, proj_term = stage(one_sums, proj_term)
    one_parts = plane_parts(one_sums)
    up_grad = stage(up_grad, one_parts)[0]
    up_grad = lax.all_to_all(
        up_grad.reshape(2 * depth, wrows, chips * frows),
        BOTH,
        0,
        0,
        tiled=True,
        axis_index_groups=chip_devices(),
    )

    def qkv_parts(*gate):
        halves = stage(mixed_halves, gate)[0]
        term = plain_over_rows(normed_one, halves)
        term = term.reshape(count, depth, wrows, wide_cols).transpose(1, 0, 2, 3)
        return column_parts(term.reshape(depth * count * wrows, wide_cols))

    grad_one, qkv_term = plane_sum(one_parts, qkv_parts)
    qkv_near = column_near(qkv_term)
    scaled_one, inverse_one = normalize(own_rows)
    gain_one_term = jnp.sum(grad_one * scaled_one, 0)
    shift_one_term = jnp.sum(grad_one, 0)
    held = (grad_one, qkv_term, qkv_near, up_grad, proj_term, out_sum)
    gain_one_term, shift_one_term, held = stage(gain_one_term, shift_one_term, held)
    grad_one, qkv_term, qkv_near, up_grad, proj_term, out_sum = held

    result = middle + out_sum.astype(F32) + dbias
    layer_out = jnp.where(live, result, 0.0).astype(BF)
    qkv_grad = column_far(qkv_term, qkv_near).astype(BF)
    qkv_grad = qkv_grad.reshape(count, wrows, wide_cols)
    input_grad = grad_middle + norm_backward(grad_one, scaled_one, inverse_one, gain_one)
    up_grad = (
        up_grad.reshape(2 * depth, wrows, chips, frows)
        .transpose(1, 2, 0, 3)
        .reshape(wrows, hidden)
        .astype(F32)
    )
    qkv_grad = lax.all_to_all(qkv_grad, "ctx", 0, 0, tiled=True).transpose(1, 0, 2).astype(F32)
    kinds = jnp.sum(qkv_grad[:, :, qcols:].reshape(wrows, chips, 2 * HD), 1)
    qkv_grad = jnp.concatenate([qkv_grad[:, :, :qcols].reshape(wrows, width), kinds], 1)

    mixed_term = jnp.sum(grad_mixed.astype(F32), 0)
    vbias_term = jnp.where(core == 1, mixed_term[qcols:], 0.0).reshape(count * depth, -1)
    vbias_term = jnp.pad(vbias_term, ((0, 0), (0, wrows - vbias_term.shape[1]))).reshape(-1)
    ubias_term = ubias_term.reshape(chips, 1, frows)
    ubias_term = jnp.where(jnp.arange(2)[None, :, None] == core, ubias_term, 0.0)
    terms = [pbias_term, gain_two_term, shift_two_term, dbias_term, vbias_term]
    early = jnp.stack(terms + [jnp.zeros_like(vbias_term)] * 3)
    early = early.reshape(8, count, -1)
    ub = jnp.pad(ubias_term.reshape(1, count, frows), ((0, 7), (0, 0), (0, 0)))
    early, ub = early.transpose(1, 0, 2), ub.transpose(1, 0, 2)
    late = jnp.stack([gain_one_term, shift_one_term]).reshape(2, count, -1).transpose(1, 0, 2)
    late = jnp.pad(late, ((0, 0), (5, 1), (0, 0)))
    block = late.shape[2]
    first = lax.all_to_all(
        jnp.concatenate([early + late, ub], 2), "ctx", 0, 0, tiled=True
    )
    down_grad, proj_term = stage(down_grad, proj_term, first)[:2]
    proj_grad = lax.psum_scatter(proj_term, "fsdp", scatter_dimension=0, tiled=True)
    proj_grad, down_grad = proj_grad.astype(F32), down_grad.astype(F32)
    first = jnp.sum(first, 0)
    ubias_grad = first[0, block:]
    second = first[:, :block] + jnp.pad(mixed_term[None, :qcols], ((7, 0), (0, 0)))
    second = second.reshape(8, depth, wrows).transpose(1, 0, 2)
    second = lax.all_to_all(second, "fsdp", 0, 0, tiled=True)
    second = jnp.sum(second, 0)
    wide_grads = [second[i] for i in (5, 6, 0, 1, 2, 3)]
    vbias_grad = second[4, : value_bias.shape[0]]
    qbias_grad = second[7]
    return (
        layer_out[None],
        input_grad[None],
        wide_grads[0],
        wide_grads[1],
        qkv_grad,
        qbias_grad,
        vbias_grad,
        proj_grad,
        wide_grads[2],
        wide_grads[3],
        wide_grads[4],
        up_grad,
        ubias_grad,
        down_grad,
        wide_grads[5],
    )


def solution(mesh):
    rows = P("fsdp", "ctx", None)
    vector = P(BOTH)
    matrix = P(BOTH, None)
    return jax.shard_map(
        body,
        mesh=mesh,
        in_specs=(
            rows, rows, P("fsdp"), vector, vector, matrix, vector, vector, matrix,
            vector, vector, vector, matrix, vector, matrix, vector,
        ),
        out_specs=(
            rows, rows, vector, vector, matrix, vector, vector, matrix, vector,
            vector, vector, matrix, vector, matrix, vector,
        ),
        check_vma=False,
    )
```

```python
import functools
import math

import jax
import jax.numpy as jnp
from jax import lax
from jax.experimental import pallas as pl
from jax.experimental.pallas import tpu as pltpu
from jax.sharding import PartitionSpec as P

HEADS = 16
HD = 128
EPS = 1e-05
NEG = -1e30
TILE = 512
BOTH = ("ctx", "fsdp")
BF = jnp.bfloat16
F32 = jnp.float32


def dot(a, b, da, db):
    return lax.dot_general(
        a, b, (((da,), (db,)), ((), ())), preferred_element_type=F32
    )


def normalize(values):
    center = values - jnp.mean(values, -1, keepdims=True)
    inverse = lax.rsqrt(jnp.mean(center * center, -1, keepdims=True) + EPS)
    return center * inverse, inverse


def norm_backward(grad, scaled, inverse, gain):
    inner = grad * gain
    return inverse * (
        inner
        - jnp.mean(inner, -1, keepdims=True)
        - scaled * jnp.mean(inner * scaled, -1, keepdims=True)
    )


def gelu(values):
    return jax.nn.gelu(values, approximate=True)


def attend_kernel(q_ref, k_ref, v_ref, row_limit_ref, key_pos_ref, out_ref):
    scale = 1.0 / math.sqrt(HD)
    allowed = key_pos_ref[...] <= row_limit_ref[...]
    scores = jnp.where(allowed, dot(q_ref[...], k_ref[...], 1, 1) * scale, NEG)
    top = jnp.max(scores, -1, keepdims=True)
    expo = jnp.exp(scores - top)
    probs = expo * (1.0 / jnp.sum(expo, -1, keepdims=True))
    out_ref[...] = dot(probs.astype(BF), v_ref[...], 1, 0).astype(BF)


def attend(queries, keys, values, limit, pos):
    rows = min(TILE, queries.shape[0])
    count = queries.shape[1] // HD - 1
    tile = pl.BlockSpec((rows, HD), lambda h, i: (i, h))
    whole = pl.BlockSpec(keys.shape, lambda h, i: (0, 0))
    return pl.pallas_call(
        attend_kernel,
        grid=(count, queries.shape[0] // rows),
        in_specs=[
            tile,
            whole,
            whole,
            pl.BlockSpec((rows, 1), lambda h, i: (i, 0)),
            pl.BlockSpec((1, keys.shape[0]), lambda h, i: (0, 0)),
        ],
        out_specs=tile,
        out_shape=jax.ShapeDtypeStruct((queries.shape[0], count * HD), BF),
        cost_estimate=pl.CostEstimate(flops=0, bytes_accessed=0, transcendentals=0),
        name="attend",
    )(queries, keys, values, limit[:, None], pos[None, :])


def attend_back_kernel(
    q_ref, k_ref, v_ref, grad_ref, row_limit_ref, key_pos_ref, gq_ref, gk_ref, gv_ref
):
    scale = 1.0 / math.sqrt(HD)

    @pl.when((pl.program_id(0) == 0) & (pl.program_id(1) == 0))
    def _():
        gk_ref[...] = jnp.zeros_like(gk_ref)
        gv_ref[...] = jnp.zeros_like(gv_ref)

    q, k, v, grad = q_ref[...], k_ref[...], v_ref[...], grad_ref[...]
    allowed = key_pos_ref[...] <= row_limit_ref[...]
    scores = jnp.where(allowed, dot(k, q, 1, 1) * scale, NEG)
    top = jnp.max(scores, 0, keepdims=True)
    expo = jnp.exp(scores - top)
    probs = expo * (1.0 / jnp.sum(expo, 0, keepdims=True))
    gv_ref[...] += dot(probs.astype(BF), grad, 1, 0)
    grad_probs = dot(v, grad, 1, 1)
    delta = jnp.sum(probs * grad_probs, 0, keepdims=True)
    grad_scores = (probs * (grad_probs - delta)).astype(BF)
    gk_ref[...] += dot(grad_scores, q, 1, 0) * scale
    gq_ref[...] = (dot(grad_scores, k, 0, 0) * scale).astype(BF)


def attend_back(queries, keys, values, grads, limit, pos):
    rows = min(TILE, queries.shape[0])
    count = queries.shape[1] // HD - 1
    tile = pl.BlockSpec((rows, HD), lambda h, i: (i, h))
    whole = pl.BlockSpec(keys.shape, lambda h, i: (0, 0))
    return pl.pallas_call(
        attend_back_kernel,
        grid=(count, queries.shape[0] // rows),
        in_specs=[
            tile,
            whole,
            whole,
            tile,
            pl.BlockSpec((1, rows), lambda h, i: (0, i)),
            pl.BlockSpec((keys.shape[0], 1), lambda h, i: (0, 0)),
        ],
        out_specs=[tile, whole, whole],
        out_shape=[
            jax.ShapeDtypeStruct((queries.shape[0], count * HD), BF),
            jax.ShapeDtypeStruct(keys.shape, F32),
            jax.ShapeDtypeStruct(keys.shape, F32),
        ],
        cost_estimate=pl.CostEstimate(flops=0, bytes_accessed=0, transcendentals=0),
        name="attend_back",
    )(queries, keys, values, grads, limit[None, :], pos[:, None])


def stage(*values):
    return lax.optimization_barrier(values)


def call(kernel, grid, in_specs, out_specs, out_shape, name):
    return pl.pallas_call(
        kernel,
        grid=grid,
        in_specs=in_specs,
        out_specs=out_specs,
        out_shape=out_shape,
        cost_estimate=pl.CostEstimate(flops=0, bytes_accessed=0, transcendentals=0),
        name=name,
    )


def multiply_kernel(dim, a_ref, b_ref, out_ref):
    out_ref[...] = dot(a_ref[...], b_ref[...], 1, dim).astype(out_ref.dtype)


def multiply(a, b, dim, dtype=F32):
    rows, depth = a.shape
    columns = b.shape[1 - dim]
    tile = min(512, columns)
    if dim:
        b_spec = pl.BlockSpec((tile, depth), lambda j: (j, 0))
    else:
        b_spec = pl.BlockSpec((depth, tile), lambda j: (0, j))
    return call(
        functools.partial(multiply_kernel, dim),
        (columns // tile,),
        [pl.BlockSpec((rows, depth), lambda j: (0, 0)), b_spec],
        pl.BlockSpec((rows, tile), lambda j: (0, j)),
        jax.ShapeDtypeStruct((rows, columns), dtype),
        "multiply",
    )(a, b)


def over_rows_kernel(a0_ref, a1_ref, b0_ref, b1_ref, out_ref):
    total = dot(a0_ref[...], b0_ref[...], 0, 0) + dot(a1_ref[...], b1_ref[...], 0, 0)
    out_ref[...] = total.astype(BF)


def dot_over_rows(lefts, rights):
    rows, height = lefts[0].shape
    width = rights[0].shape[1]
    tile = min(256, height)
    left = pl.BlockSpec((rows, tile), lambda i: (0, i))
    right = pl.BlockSpec((rows, width), lambda i: (0, 0))
    return call(
        over_rows_kernel,
        (height // tile,),
        [left, left, right, right],
        pl.BlockSpec((tile, width), lambda i: (i, 0)),
        jax.ShapeDtypeStruct((height, width), BF),
        "over_rows",
    )(*lefts, *rights)


def plain_over_rows(lefts, rights):
    return (dot(lefts[0], rights[0], 0, 0) + dot(lefts[1], rights[1], 0, 0)).astype(BF)


def hidden_kernel(x0_ref, x1_ref, w_ref, bias_ref, g0_ref, g1_ref, a0_ref, a1_ref, o0_ref, o1_ref):
    root, cubic = math.sqrt(2.0 / math.pi), 0.044715
    halves = (x0_ref, g0_ref, a0_ref, o0_ref), (x1_ref, g1_ref, a1_ref, o1_ref)
    for x_ref, grad_ref, active_ref, out_ref in halves:
        u = dot(x_ref[...], w_ref[...], 1, 0) + bias_ref[...]
        square = u * u
        t = jnp.tanh(root * u * (1.0 + cubic * square))
        active_ref[...] = (0.5 * u * (1.0 + t)).astype(BF)
        slope = 0.5 * (1.0 + t) + 0.5 * u * (1.0 - t * t) * (root * (1.0 + 3.0 * cubic * square))
        out_ref[...] = (grad_ref[...] * slope).astype(BF)


def hidden_layer(halves, weight, bias, grads):
    count, width = halves[0].shape
    columns = weight.shape[1]
    tile = min(256, columns)
    whole = pl.BlockSpec((count, width), lambda j: (0, 0))
    piece = pl.BlockSpec((count, tile), lambda j: (0, j))
    a0, a1, o0, o1 = call(
        hidden_kernel,
        (columns // tile,),
        [
            whole,
            whole,
            pl.BlockSpec((width, tile), lambda j: (0, j)),
            pl.BlockSpec((1, tile), lambda j: (0, j)),
            piece,
            piece,
        ],
        [piece] * 4,
        [jax.ShapeDtypeStruct((count, columns), BF)] * 4,
        "hidden_layer",
    )(*halves, weight, bias[None], *grads)
    return (a0, a1), (o0, o1)


def exchange(value, mask):
    count = lax.axis_size("ctx")
    return lax.ppermute(value, "ctx", [(i, i ^ mask) for i in range(count)])


def chip_groups():
    count = lax.axis_size("ctx")
    return [list(range(core, count, 2)) for core in range(2)]


def chip_devices():
    width = 2 * lax.axis_size("fsdp")
    total = lax.axis_size("ctx") * lax.axis_size("fsdp")
    return [list(range(at, at + width)) for at in range(0, total, width)]


def plane_direct(value):
    chips = lax.axis_size("ctx") // 2
    return [value] + [exchange(value, 2 * k) for k in range(1, chips)]


def both_cores(own):
    return own, exchange(own, 1)


def core_sum(lefts, weight, dim):
    other, early = stage(dot(lefts[1], weight, 1, dim).astype(BF), lefts[0])
    return stage(dot(early, weight, 1, dim), exchange(other, 1))


def plane_parts(halves):
    own, other = halves
    chips = lax.axis_size("ctx") // 2
    rows = own.shape[0] // chips
    parts = [
        own[k * rows : (k + 1) * rows] + other[k * rows : (k + 1) * rows].astype(F32)
        for k in range(chips)
    ]
    return [parts[0]] + [piece.astype(BF) for piece in parts[1:]]


def plane_sum(parts, fill=None):
    chips = lax.axis_size("ctx") // 2
    arrived = [exchange(parts[k], 2 * k) for k in range(1, chips - 1)]
    filled = fill(*parts) if fill else ()
    last = stage(parts[chips - 1], filled)[0]
    total = parts[0]
    for piece in arrived + [exchange(last, 2 * chips - 2)]:
        total = total + piece.astype(F32)
    return total, filled


def turned(value, by):
    depth = lax.axis_size("fsdp")
    return lax.ppermute(value, "fsdp", [(i, (i + by) % depth) for i in range(depth)])


def slot(s):
    depth = lax.axis_size("fsdp")
    return (lax.axis_index("fsdp") - s) % depth


def near_rows(value):
    depth = lax.axis_size("fsdp")
    return {s: turned(value, s) for s in range(1, depth) if s != depth // 2}


def far_rows(value, near):
    depth = lax.axis_size("fsdp")
    pieces = {0: value, **near, depth // 2: turned(value, depth // 2)}
    rows = jnp.zeros((depth,) + value.shape, value.dtype)
    for s, piece in pieces.items():
        rows = lax.dynamic_update_slice(rows, piece[None], (slot(s), 0, 0))
    return rows.reshape(depth * value.shape[0], value.shape[1])


def column_parts(own, other=None):
    depth = lax.axis_size("fsdp")
    rows = own.shape[0] // depth
    parts = []
    for s in range(depth):
        part = lax.dynamic_slice_in_dim(own, slot(s) * rows, rows, 0)
        if other is not None:
            theirs = lax.dynamic_slice_in_dim(other, slot(s) * rows, rows, 0)
            part = part + theirs.astype(F32)
        parts.append(part.astype(BF) if s else part.astype(F32))
    return parts


def column_near(parts):
    depth = len(parts)
    return [parts[0]] + [turned(parts[s], -s) for s in range(1, depth) if s != depth // 2]


def column_far(parts, near):
    middle = len(parts) // 2
    total = turned(parts[middle], -middle).astype(F32)
    for piece in near:
        total = total + piece.astype(F32)
    return total


def lay_out(vectors, width):
    row, column, laid, places = 0, 0, 0, []
    for v in vectors:
        n = v.shape[0]
        if column + n > width:
            row, column = row + 1, 0
        places.append((row, column, n))
        laid = laid + jnp.pad(v[None], ((row, 7 - row), (column, width - column - n)))
        column += -(-n // 128) * 128
    return laid, places


def body(
    hidden_in,
    out_cotangent,
    seq_lengths,
    first_gain,
    first_shift,
    qkv_weight,
    query_bias,
    value_bias,
    proj_weight,
    proj_bias,
    second_gain,
    second_shift,
    up_weight,
    up_bias,
    down_weight,
    down_bias,
):
    count, depth = lax.axis_size("ctx"), lax.axis_size("fsdp")
    chips = count // 2
    at, level = lax.axis_index("ctx"), lax.axis_index("fsdp")
    core, chip = at % 2, at // 2
    span, width = hidden_in.shape[1:]
    wrows = qkv_weight.shape[0]
    hidden = up_weight.shape[1]
    frows = down_weight.shape[0]
    share = HEADS // count
    qcols = share * HD
    wide_cols = qcols + HD
    total = span * count
    length = seq_lengths[0]
    positions = at * span + jnp.arange(span, dtype=jnp.int32)
    live = (positions < length)[:, None]

    small = [
        first_gain,
        first_shift,
        query_bias,
        value_bias,
        proj_bias,
        second_gain,
        second_shift,
        up_bias,
        down_bias,
    ]
    packed, places = lay_out(small, wide_cols)
    qpart = qkv_weight[:, :width].reshape(wrows, count, qcols).transpose(1, 0, 2)
    kvpart = qkv_weight[:, width:].reshape(wrows, 2, HD).transpose(1, 0, 2)
    kvpart = jnp.broadcast_to(kvpart[None], (chips, 2, wrows, HD)).reshape(count, wrows, HD)
    outgoing = jnp.concatenate(
        [
            jnp.concatenate([qpart, kvpart], 2),
            jnp.broadcast_to(packed[None], (count,) + packed.shape),
        ],
        1,
    )
    incoming = lax.all_to_all(outgoing, "ctx", 0, 0, tiled=True)
    incoming, hidden_own, upstream = stage(incoming, hidden_in[0], out_cotangent[0])

    attn_all = lax.all_gather(incoming, "fsdp", axis=0)
    row_pieces = plane_direct(hidden_own)
    row_halves = both_cores(jnp.concatenate(row_pieces, 0))
    down_pieces = plane_direct(stage(down_weight, row_pieces)[0])
    own_rows = hidden_own.astype(F32)
    upstream = jnp.where(live, upstream.astype(F32), 0.0)
    grad_mlp_own = upstream.astype(BF)
    attn_all, row_halves, grad_mlp_own, proj_own, up_own = stage(
        attn_all, row_halves, grad_mlp_own, proj_weight, up_weight
    )

    proj_local = lax.all_gather(proj_own, "fsdp", axis=0, tiled=True)
    mlp_rows = lax.all_gather(grad_mlp_own, "fsdp", axis=0, tiled=True)
    up_parts = (
        up_own.reshape(wrows, chips, 2 * depth, frows)
        .transpose(2, 0, 1, 3)
        .reshape(2 * depth, wrows, chips * frows)
    )
    up_parts = lax.all_to_all(
        up_parts, BOTH, 0, 0, tiled=True, axis_index_groups=chip_devices()
    ).reshape(2 * depth * wrows, chips * frows)
    attn_rows = attn_all.transpose(1, 0, 2, 3)
    qkv_local = attn_rows[:, :, :wrows].reshape(width, wide_cols)
    table = attn_rows[:, :, wrows:].reshape(count * depth, 8, wide_cols)
    vectors = [table[:, r, c : c + n].reshape(-1).astype(F32) for r, c, n in places]
    gain_one, shift_one, qbias, vbias, pbias, gain_two, shift_two, ubias, dbias = vectors
    ubias = lax.dynamic_slice(
        ubias.reshape(chips, 2 * depth, frows), (0, core * depth + level, 0), (chips, 1, frows)
    ).reshape(-1)
    bias_one = jnp.concatenate(
        [
            lax.dynamic_slice(qbias, (at * qcols,), (qcols,)),
            jnp.where(core == 1, vbias, 0.0),
        ]
    )
    normed_one = [
        (normalize(half.astype(F32))[0] * gain_one + shift_one).astype(BF) for half in row_halves
    ]
    mixed = jnp.concatenate([dot(half, qkv_local, 1, 0) for half in normed_one], 0)
    queries = (mixed + bias_one).astype(BF)
    mine = queries[:, qcols:]
    theirs = jnp.roll(exchange(mine, 1), total // 2, 0)
    keys = jnp.where(core == 0, mine, theirs)
    values = jnp.where(core == 0, theirs, mine)
    base = jnp.stack([at ^ (2 * k + j) for j in range(2) for k in range(chips)]) * span
    pos = (base[:, None] + jnp.arange(span, dtype=jnp.int32)[None]).reshape(total)
    limit = jnp.minimum(pos, length - 1)
    attended = attend(queries, keys, values, limit, pos)
    held = (pbias, gain_two, shift_two, ubias, dbias)
    attended, up_parts, held, proj_local, down_pieces = stage(
        attended, up_parts, held, proj_local, down_pieces
    )
    pbias, gain_two, shift_two, ubias, dbias = held

    attended_halves = attended[: total // 2], attended[total // 2 :]
    down_local = jnp.zeros((chips, frows, width), BF)
    for k, piece in enumerate(down_pieces):
        down_local = lax.dynamic_update_slice(down_local, piece[None], (chip ^ k, 0, 0))
    down_local = down_local.reshape(chips * frows, width)
    branch, _ = plane_sum(plane_parts(core_sum(attended_halves, proj_local, 0)))
    middle = own_rows + branch + pbias
    scaled_two, inverse_two = normalize(middle)
    normed_two_own = (scaled_two * gain_two + shift_two).astype(BF)
    normed_two_own, down_local, up_parts, mlp_rows = stage(
        normed_two_own, down_local, up_parts, mlp_rows
    )

    up_local = lax.all_gather(
        up_parts, "ctx", axis=0, tiled=True, axis_index_groups=chip_groups()
    )

    near = near_rows(normed_two_own)
    mlp_halves = both_cores(mlp_rows)
    grad_active = [multiply(half, down_local, 1) for half in mlp_halves]
    near, normed_value, mlp_halves, grad_active = stage(
        near, normed_two_own, mlp_halves, grad_active
    )
    normed_rows = far_rows(normed_value, near)
    normed_rows = stage(normed_rows)[0]

    normed_halves = both_cores(normed_rows)
    active, grad_before = hidden_layer(normed_halves, up_local, ubias, grad_active)

    def chip_sum(term):
        return lax.psum_scatter(
            term, "ctx", scatter_dimension=0, tiled=True, axis_index_groups=chip_groups()
        )

    two_parts = column_parts(*core_sum(grad_before, up_local, 1))

    held = stage(normed_halves, grad_before, active, mlp_halves, two_parts)
    normed, grads, acts, mlps = held[:4]
    out_other = multiply(acts[1], down_local, 0, BF)
    out_own = multiply(acts[0], down_local, 0)
    up_term = dot_over_rows(normed, grads)
    near, two_parts, up_term, out_own, out_other = stage(
        column_near(two_parts), two_parts, up_term, out_own, out_other
    )
    out_term = (out_own + exchange(out_other, 1).astype(F32)).astype(BF)
    up_grad = chip_sum(up_term)
    acts, mlps, grads = stage(acts, mlps, grads, near)[:3]
    down_term = dot_over_rows(acts, mlps)
    ubias_term = jnp.sum(grads[0].astype(F32), 0) + jnp.sum(grads[1].astype(F32), 0)
    grad_two = column_far(two_parts, near)
    gain_two_term = jnp.sum(grad_two * scaled_two, 0)
    shift_two_term = jnp.sum(grad_two, 0)
    grad_middle = upstream + norm_backward(grad_two, scaled_two, inverse_two, gain_two)
    grad_branch_own = grad_middle.astype(BF)
    grad_branch_own, out_term, down_term, ubias_term = stage(
        grad_branch_own, out_term, down_term, ubias_term
    )
    out_sum = lax.psum_scatter(out_term, "fsdp", scatter_dimension=0, tiled=True)

    branch_halves = both_cores(jnp.concatenate(plane_direct(grad_branch_own), 0))
    pbias_term = jnp.sum(grad_branch_own.astype(F32), 0)
    dbias_term = jnp.sum(grad_mlp_own.astype(F32), 0)
    branch_halves, pbias_term, dbias_term, up_grad = stage(
        branch_halves, pbias_term, dbias_term, up_grad
    )

    grad_attended = jnp.concatenate(
        [dot(half, proj_local, 1, 1) for half in branch_halves], 0
    ).astype(BF)
    grad_queries, grad_keys, grad_values = attend_back(
        queries, keys, values, grad_attended, limit, pos
    )
    given = jnp.where(core == 0, grad_values, grad_keys).astype(BF)
    given = jnp.roll(exchange(given, 1), total // 2, 0).astype(F32)
    grad_kind = (jnp.where(core == 0, grad_keys, grad_values) + given).astype(BF)
    grad_mixed = jnp.concatenate([grad_queries, grad_kind], 1)

    grad_mixed, down_term = stage(grad_mixed, down_term)
    down_grad = chip_sum(down_term)

    mixed_halves = grad_mixed[: total // 2], grad_mixed[total // 2 :]
    proj_term = plain_over_rows(attended_halves, branch_halves)
    one_sums = core_sum(mixed_halves, qkv_local, 1)
    one_sums, proj_term = stage(one_sums, proj_term)
    one_parts = plane_parts(one_sums)
    up_grad = stage(up_grad, one_parts)[0]
    up_grad = lax.all_to_all(
        up_grad.reshape(2 * depth, wrows, chips * frows),
        BOTH,
        0,
        0,
        tiled=True,
        axis_index_groups=chip_devices(),
    )

    def qkv_parts(*gate):
        halves = stage(mixed_halves, gate)[0]
        term = plain_over_rows(normed_one, halves)
        term = term.reshape(count, depth, wrows, wide_cols).transpose(1, 0, 2, 3)
        return column_parts(term.reshape(depth * count * wrows, wide_cols))

    grad_one, qkv_term = plane_sum(one_parts, qkv_parts)
    qkv_near = column_near(qkv_term)
    scaled_one, inverse_one = normalize(own_rows)
    gain_one_term = jnp.sum(grad_one * scaled_one, 0)
    shift_one_term = jnp.sum(grad_one, 0)
    held = (grad_one, qkv_term, qkv_near, up_grad, proj_term, out_sum)
    gain_one_term, shift_one_term, held = stage(gain_one_term, shift_one_term, held)
    grad_one, qkv_term, qkv_near, up_grad, proj_term, out_sum = held

    result = middle + out_sum.astype(F32) + dbias
    layer_out = jnp.where(live, result, 0.0).astype(BF)
    qkv_grad = column_far(qkv_term, qkv_near).astype(BF)
    qkv_grad = qkv_grad.reshape(count, wrows, wide_cols)
    input_grad = grad_middle + norm_backward(grad_one, scaled_one, inverse_one, gain_one)
    up_grad = (
        up_grad.reshape(2 * depth, wrows, chips, frows)
        .transpose(1, 2, 0, 3)
        .reshape(wrows, hidden)
        .astype(F32)
    )
    qkv_grad = lax.all_to_all(qkv_grad, "ctx", 0, 0, tiled=True).transpose(1, 0, 2).astype(F32)
    kinds = jnp.sum(qkv_grad[:, :, qcols:].reshape(wrows, chips, 2 * HD), 1)
    qkv_grad = jnp.concatenate([qkv_grad[:, :, :qcols].reshape(wrows, width), kinds], 1)

    mixed_term = jnp.sum(grad_mixed.astype(F32), 0)
    vbias_term = jnp.where(core == 1, mixed_term[qcols:], 0.0).reshape(count * depth, -1)
    vbias_term = jnp.pad(vbias_term, ((0, 0), (0, wrows - vbias_term.shape[1]))).reshape(-1)
    ubias_term = ubias_term.reshape(chips, 1, frows)
    ubias_term = jnp.where(jnp.arange(2)[None, :, None] == core, ubias_term, 0.0)
    terms = [pbias_term, gain_two_term, shift_two_term, dbias_term, vbias_term]
    early = jnp.stack(terms + [jnp.zeros_like(vbias_term)] * 3)
    early = early.reshape(8, count, -1)
    ub = jnp.pad(ubias_term.reshape(1, count, frows), ((0, 7), (0, 0), (0, 0)))
    early, ub = early.transpose(1, 0, 2), ub.transpose(1, 0, 2)
    late = jnp.stack([gain_one_term, shift_one_term]).reshape(2, count, -1).transpose(1, 0, 2)
    late = jnp.pad(late, ((0, 0), (5, 1), (0, 0)))
    block = late.shape[2]
    first = lax.all_to_all(
        jnp.concatenate([early + late, ub], 2), "ctx", 0, 0, tiled=True
    )
    down_grad, proj_term = stage(down_grad, proj_term, first)[:2]
    proj_grad = lax.psum_scatter(proj_term, "fsdp", scatter_dimension=0, tiled=True)
    proj_grad, down_grad = proj_grad.astype(F32), down_grad.astype(F32)
    first = jnp.sum(first, 0)
    ubias_grad = first[0, block:]
    second = first[:, :block] + jnp.pad(mixed_term[None, :qcols], ((7, 0), (0, 0)))
    second = second.reshape(8, depth, wrows).transpose(1, 0, 2)
    second = lax.all_to_all(second, "fsdp", 0, 0, tiled=True)
    second = jnp.sum(second, 0)
    wide_grads = [second[i] for i in (5, 6, 0, 1, 2, 3)]
    vbias_grad = second[4, : value_bias.shape[0]]
    qbias_grad = second[7]
    return (
        layer_out[None],
        input_grad[None],
        wide_grads[0],
        wide_grads[1],
        qkv_grad,
        qbias_grad,
        vbias_grad,
        proj_grad,
        wide_grads[2],
        wide_grads[3],
        wide_grads[4],
        up_grad,
        ubias_grad,
        down_grad,
        wide_grads[5],
    )


def solution(mesh):
    rows = P("fsdp", "ctx", None)
    vector = P(BOTH)
    matrix = P(BOTH, None)
    return jax.shard_map(
        body,
        mesh=mesh,
        in_specs=(
            rows, rows, P("fsdp"), vector, vector, matrix, vector, vector, matrix,
            vector, vector, vector, matrix, vector, matrix, vector,
        ),
        out_specs=(
            rows, rows, vector, vector, matrix, vector, vector, matrix, vector,
            vector, vector, matrix, vector, matrix, vector,
        ),
        check_vma=False,
    )
```
